128 devices in a mesh: row: 8 (over y, core), col: 16 (over x, z).
Axes of the slice: x: 4, y: 4, z: 4, core: 2. Of those that a mesh axis runs over, the one named last changes fastest.
Arguments:
- strip_columns: float32 [4096, 32, 256], P(('row', 'col')), may hold values from -0.0048828125 to 0.0048828125
- tile_columns: float32 [4096, 4, 32, 256], P(('row', 'col')), may hold values from -6 to 6
- barrier_weights: float32 [4096, 32], P(('row', 'col')), may hold values from 0.01 to 100
- column_counts: int32 [4096], P(('row', 'col')), may hold values from 1 to 32
- tile_lists: int32 [4096, 4], P(('row', 'col')), may hold values from 0 to 127, all different within a row; in each aligned block of 32 rows (0 to 31, 32 to 63, ...) at most 2 rows name the same one
Outputs:
- panel_factor: float32 [256, 256], replicated
- strip_update: float32 [256, 32768], P(None, ('row', 'col'))
The draws below stay inside these ranges and needn't reach their ends.
Inputs may be any that keep to these rules, and one draw needn't show every extreme that they name: `tile_lists`: each block lists 4 different column tiles; among the 32 blocks of one device no tile is listed more than 2 times, and in some device one tile is listed exactly 2 times.
All inputs are finite; a program needn't handle non-finite values.
Results may differ from the reference program's by a relative error of at most 0.0001.
Values sent between devices are 32-bit elements; how exact they have to be, the bound alone decides.
A program may use at most 192 MiB of HBM per device.

```python
import math
import jax
import jax.numpy as jnp
import numpy as np
from jax import lax

TILE = 256
REST = 32768
NB = 32
TOUCH = 4
BLK_DEV = 32
BLOCKS = 4096
CT = 256
CAP = 2
N_ROW = 8
N_COL = 16


def plant(result, stream_key, low, high):
    longest = result.shape.index(max(result.shape))
    spots = []
    for shift in (0, 1):
        where = [jax.random.randint(jax.random.fold_in(stream_key, axis), (), 0, length) for axis, length in enumerate(result.shape)]
        where[longest] = (where[longest] + shift) % result.shape[longest]
        spots.append(tuple(where))
    return result.at[spots[0]].set(low).at[spots[1]].set(high)


def shard_levels(own_key, extent, split, least, high):
    factor_of, own = 1.0, jax.random.fold_in(own_key, 6)
    for dim, shards_of in split:
        draws = jnp.exp(jax.random.uniform(jax.random.fold_in(own, dim), (shards_of,), jnp.float32, least / len(split), high / len(split)))
        factor_of = factor_of * jnp.repeat(draws, extent[dim] // shards_of).reshape([-1 if axis == dim else 1 for axis in range(len(extent))])
    return factor_of


def assign_block(own_key, own, number, rows, count, top, bound, lean):
    ranking = jax.random.permutation(own_key, count)
    crowded, common = portions_of(count, rows * top, bound, lean, True), portions_of(count, rows * top, bound, lean, False)
    places = jnp.arange(count)

    def named(lengths, turn):
        used = int((lengths > 0).sum())
        fixed = max(1, used // 4)
        moved = fixed + (places - fixed + turn * (used - fixed)) % max(1, count - fixed)
        return jnp.zeros((count,), jnp.int32).at[ranking[jnp.where(places < fixed, places, moved)]].set(jnp.asarray(lengths, jnp.int32))

    lengths = jnp.where(number % 4 == 0, named(crowded, number // 4), named(common, number - number // 4 - 1))
    mixed = jax.random.permutation(jax.random.fold_in(own, 3), count)
    source_of, taker = mixed[0:count // 2 * 2:2], mixed[1:count // 2 * 2:2]
    margin = jnp.minimum(lengths[source_of] - 1, bound - lengths[taker]) // 2
    margin = jnp.where((source_of == ranking[0]) | (taker == ranking[0]) | (lengths[taker] == 0), 0, jnp.maximum(margin, 0))
    moved = jax.random.randint(jax.random.fold_in(own, 4), (count // 2,), 0, 1 << 20) % (margin + 1)
    lengths = lengths.at[source_of].add(-moved).at[taker].add(moved)
    items = jnp.searchsorted(jnp.cumsum(lengths), jnp.arange(rows * top), side="right").astype(jnp.int32)
    listing = items.reshape(top, rows).T
    listing = listing[jax.random.permutation(jax.random.fold_in(own, 1), rows)]
    turn = jax.random.randint(jax.random.fold_in(own, 2), (rows, 1), 0, top)
    return jnp.take_along_axis(listing, (jnp.arange(top)[None, :] + turn) % top, axis=1)


def portions_of(number_of, total, limit, slope, full):
    loads = [(1 << 20) // math.isqrt(standing ** slope) + 1 for standing in range(1, number_of + 1)]
    largest = limit if full else min(limit, max(-(-total // number_of), total * loads[0] // sum(loads)))
    least = 1 if total - largest >= number_of - 1 else 0
    given, surplus = [largest] + [least] * (number_of - 1), total - largest - least * (number_of - 1)
    while surplus > 0:
        free = [i for i in range(1, number_of) if given[i] < largest] or [i for i in range(1, number_of) if given[i] < limit]
        mass, left = sum([loads[i] for i in free]), surplus
        for i in free:
            more = min(limit - given[i], max(1, left * loads[i] // mass), surplus)
            given[i] = given[i] + more
            surplus = surplus - more
    return np.array(given)


def bell_draw(rng, dims, spread, reach, pieces=(), kind=jnp.bfloat16):
    values = jax.random.normal(rng, dims, jnp.float32) * spread
    if len(pieces) > 0:
        values = shard_levels(rng, dims, pieces, -0.22, 0.18) * values
    return jnp.clip(values, min=-reach, max=reach).astype(kind)


def setup_inputs(seed: int = 0) -> dict:
    splits = jax.random.split(jax.random.key(seed), 6)
    strip_columns = bell_draw(splits[0], (BLOCKS, NB, TILE), (BLOCKS * NB * 10) ** -0.5, 0.0048828125, ((0, 128),), jnp.float32)
    tile_columns = bell_draw(splits[1], (BLOCKS, TOUCH, NB, CT), 1.0, 6.0, ((0, 128),), jnp.float32)
    barrier_weights = jnp.clip(jnp.exp(math.log(100.0) - 9.2103404 * jax.random.uniform(splits[2], (BLOCKS, NB), jnp.float32) ** shard_levels(splits[2], (BLOCKS, NB), ((0, 128),), -0.2, 0.2)), 0.01, 100.0)
    column_counts = plant(jax.random.randint(splits[3], (BLOCKS,), 1, NB + 1), jax.random.fold_in(splits[3], 1), 1, NB).astype(jnp.int32)
    tile_lists_keys = jax.random.split(jax.random.fold_in(splits[4], 1), BLOCKS // BLK_DEV)
    tile_lists_turns = jax.random.permutation(jax.random.fold_in(splits[4], 3), BLOCKS // BLK_DEV)
    tile_lists = jax.vmap(lambda own, number: assign_block(jax.random.fold_in(splits[4], 2), own, number, BLK_DEV, N_ROW * N_COL, TOUCH, CAP, 2))(tile_lists_keys, tile_lists_turns).reshape((BLOCKS, TOUCH))
    return {"strip_columns": strip_columns, "tile_columns": tile_columns, "barrier_weights": barrier_weights, "column_counts": column_counts, "tile_lists": tile_lists}


def reference(strip_columns, tile_columns, barrier_weights, column_counts, tile_lists):
    devices = N_ROW * N_COL
    own_width = REST // devices
    live_mask = jnp.arange(NB, dtype=jnp.int32)[None, :] < column_counts[:, None]
    live_weight = jnp.where(live_mask, barrier_weights, 0.0)
    scaled = strip_columns * live_weight[:, :, None]
    diagonal_block = jnp.einsum('bcr,bcs->rs', scaled, strip_columns, precision=lax.Precision.HIGHEST)
    scaled_groups = scaled.reshape(devices, BLK_DEV, NB, TILE)
    tile_groups = tile_columns.reshape(devices, BLK_DEV, TOUCH, NB, own_width)
    list_groups = tile_lists.reshape(devices, BLK_DEV, TOUCH)

    def add_group(running, inputs):
        strip_part, tile_part, target_part = inputs
        partial_value = jnp.einsum('bcr,bkcj->bkrj', strip_part, tile_part, precision=lax.Precision.HIGHEST)
        return (running.at[target_part].add(partial_value), None)
    initial = jnp.zeros((devices, TILE, own_width), strip_columns.dtype)
    summed, _ = lax.scan(add_group, initial, (scaled_groups, tile_groups, list_groups))
    linking_rest = jnp.transpose(summed, (1, 0, 2)).reshape(TILE, REST)
    panel_factor = jnp.linalg.cholesky(diagonal_block)
    strip_update = jax.scipy.linalg.solve_triangular(panel_factor, linking_rest, lower=True)
    return (panel_factor, strip_update)
```

```python
import functools

import jax
import jax.numpy as jnp
from jax import lax
from jax.experimental import pallas as pl
from jax.experimental.pallas import tpu as pltpu
from jax.sharding import PartitionSpec as P

AXES = ("row", "col")
MESH = pl.DeviceIdType.MESH
ROWS = ((0, 88), (88, 88), (176, 80))
CUT = 48
STRIDE = (16, 4, 1)
LAG = 6
RING = 8
F32 = jnp.float32


def split(x):
    high = x.astype(jnp.bfloat16)
    return high, (x - high.astype(F32)).astype(jnp.bfloat16)


def dot(a, b):
    return lax.dot_general(a, b, (((1,), (0,)), ((), ())), preferred_element_type=F32)


def kernel(
    item_ref, weight_ref, strip_ref, tile_ref, sum_ref, diagonal_ref,
    strip, tile, left, sent, acc,
    fwd10, fwd11, fwd12, fin10, fin11, fin12,
    fwd20, fwd21, fwd22, fin20, fin21, fin22,
    fwd30, fwd31, fwd32, fin30, fin31, fin32,
    dfull, dpair, dhalf, dx, dquarter, dy, dz, dquarter2, dhalf2,
    load_sem, sib_send, sib_recv,
    fwd1_send, fwd1_recv, fin1_send, fin1_recv,
    fwd2_send, fwd2_recv, fin2_send, fin2_recv,
    fwd3_send, fwd3_recv, fin3_send, fin3_recv,
    d_send, d_recv,
):
    fwd1, fin1 = (fwd10, fwd11, fwd12), (fin10, fin11, fin12)
    fwd2, fin2 = (fwd20, fwd21, fwd22), (fin20, fin21, fin22)
    fwd3, fin3 = (fwd30, fwd31, fwd32), (fin30, fin31, fin32)
    row, col = lax.axis_index("row"), lax.axis_index("col")
    core = lax.rem(row, 2)
    place = (lax.div(row, 2), lax.div(col, 4), lax.rem(col, 4))
    blocks = strip.shape[0]

    def device(y, x, z, c):
        return (y * 2 + c, x * 4 + z)

    def peer(axis, step):
        at = list(place)
        at[axis] = lax.rem(at[axis] + step, 4)
        return device(*at, core)

    sibling = device(*place, 1 - core)

    barrier = pltpu.get_barrier_semaphore()
    partners = [peer(a, s) for a in range(3) for s in (1, 2, 3)] + [sibling]
    for partner in partners:
        pl.semaphore_signal(barrier, inc=1, device_id=partner, device_id_type=MESH)
    get_strip = pltpu.make_async_copy(strip_ref, strip, load_sem.at[0])
    get_tile = pltpu.make_async_copy(tile_ref, tile, load_sem.at[1])
    get_strip.start()
    get_tile.start()
    get_strip.wait()

    left[blocks] = jnp.zeros(left.shape[1:], left.dtype)

    def build(b, carry):
        scaled = strip[b] * weight_ref[b]
        high = scaled.astype(jnp.bfloat16).astype(F32)
        low = scaled - high
        stack = jnp.concatenate([high, high, low, low], axis=0)
        left[b] = stack.T.astype(jnp.bfloat16)
        return carry

    lax.fori_loop(0, blocks, build, 0)
    get_tile.wait()
    pl.semaphore_wait(barrier, len(partners))

    def remote(src, dst, send, recv, to):
        return pltpu.make_async_remote_copy(
            src_ref=src, dst_ref=dst, send_sem=send, recv_sem=recv,
            device_id=to, device_id_type=MESH,
        )

    def product(k, c):
        at = []
        for axis in range(3):
            d = lax.rem(lax.div(k, STRIDE[axis]), 4)
            step = jnp.where(d == 0, 2, jnp.where(d == 1, 1, jnp.where(d == 2, 3, 0)))
            at.append(lax.rem(place[axis] + step, 4))
        number = ((at[0] * 2 + c) * 4 + at[1]) * 4 + at[2]
        lefts, rights = [], []
        for s in range(2):
            slot = item_ref[2 * number + s]
            lefts.append(left[lax.div(slot, 4)])
            high, low = split(tile[lax.rem(slot, tile.shape[0])])
            rights += [high, low, high, low]
        return dot(jnp.concatenate(lefts, axis=1), jnp.concatenate(rights, axis=0))

    def to_sibling(k):
        return remote(
            sent.at[lax.rem(k, RING)], acc.at[k], sib_send.at[k], sib_recv.at[k], sibling
        )

    def send_out(k, carry=0):
        @pl.when(k >= RING)
        def _():
            to_sibling(k - RING).wait_send()

        sent[lax.rem(k, RING)] = product(k, 1 - core)
        to_sibling(k).start()
        return carry

    def rows_of(p):
        return pl.ds(*ROWS[p])

    def fwd_copy(stage, p, way, k, j):
        fwd = (fwd1, fwd2)[stage - 1]
        send, recv = ((fwd1_send, fwd1_recv), (fwd2_send, fwd2_recv))[stage - 1]
        axis = (p + stage - 1) % 3
        return remote(
            acc.at[k, rows_of(p)], fwd[p].at[way, j],
            send.at[p, way, j], recv.at[p, way, j], peer(axis, (1, 3)[way]),
        )

    def fin_copy(stage, p, way, k, j):
        fin = (fin1, fin2)[stage - 1]
        send, recv = ((fin1_send, fin1_recv), (fin2_send, fin2_recv))[stage - 1]
        axis = (p + stage - 1) % 3
        return remote(
            acc.at[k, rows_of(p)], fin[p].at[way, j],
            send.at[p, way, j], recv.at[p, way, j], peer(axis, (1, 3)[way]),
        )

    def take(k, carry=0):
        to_sibling(k).wait_recv()
        acc[k] = acc[k] + product(k, core)
        digit = [lax.rem(lax.div(k, STRIDE[axis]), 4) for axis in range(3)]
        for p in range(3):
            da, db, dc = digit[p], digit[(p + 1) % 3], digit[(p + 2) % 3]
            j, f = db * 2 + lax.rem(dc, 2), db * 4 + dc

            @pl.when((da == 0) & (dc < 2))
            def _():
                fwd_copy(1, p, 0, k, j).start()

            @pl.when((da == 0) & (dc >= 2))
            def _():
                fwd_copy(1, p, 1, k, j).start()

            @pl.when((da == 1) & (dc >= 2))
            def _():
                fin_copy(1, p, 0, k, f).start()

            @pl.when((da == 2) & (dc < 2))
            def _():
                fin_copy(1, p, 1, k, f).start()

        return carry

    def both(k, carry):
        send_out(k + LAG)
        return take(k)

    def diagonal_local(b, carry):
        lefts, rights = [], []
        for s in range(2):
            lefts.append(left[2 * b + s])
            high, low = split(strip[2 * b + s])
            rights += [high, low, high, low]
        dfull[...] = dfull[...] + dot(
            jnp.concatenate(lefts, axis=1), jnp.concatenate(rights, axis=0)
        )
        return carry

    def d_copies(phase):
        py, px, pz = place
        if phase == 0:
            return [remote(dfull.at[pl.ds(128 * (1 - core), 128)], dpair, d_send.at[0, 0], d_recv.at[0, 0], sibling)]
        if phase == 6:
            return [remote(dhalf2, diagonal_ref.at[pl.ds(128 * core, 128)], d_send.at[6, 0], d_recv.at[6, 0], sibling)]
        out = []
        for o in (1, 2, 3):
            if phase == 1:
                src, dst, axis = dhalf.at[pl.ds(32 * lax.rem(px + o, 4), 32)], dx.at[o - 1], 1
            elif phase == 2:
                src, dst, axis = dquarter.at[pl.ds(8 * lax.rem(py + o, 4), 8)], dy.at[o - 1], 0
            elif phase == 3:
                src, dst, axis = dz.at[pz], dz.at[pz], 2
            elif phase == 4:
                part = pl.ds(8 * py, 8)
                src, dst, axis = dquarter2.at[part], dquarter2.at[part], 0
            else:
                part = pl.ds(32 * px, 32)
                src, dst, axis = dhalf2.at[part], dhalf2.at[part], 1
            out.append(remote(src, dst, d_send.at[phase, o - 1], d_recv.at[phase, o - 1], peer(axis, o)))
        return out

    def d_arrive(phase):
        py, px, pz = place
        for o, copy in enumerate(d_copies(phase)):
            copy.wait_recv()
        if phase == 0:
            dhalf[...] = dfull[pl.ds(128 * core, 128)] + dpair[...]
        elif phase == 1:
            dquarter[...] = dhalf[pl.ds(32 * px, 32)] + dx[0] + dx[1] + dx[2]
        elif phase == 2:
            dz[pz] = dquarter[pl.ds(8 * py, 8)] + dy[0] + dy[1] + dy[2]
        elif phase == 3:
            dquarter2[pl.ds(8 * py, 8)] = dz[0] + dz[1] + dz[2] + dz[3]
        elif phase == 4:
            dhalf2[pl.ds(32 * px, 32)] = dquarter2[...]
        elif phase == 5:
            diagonal_ref[pl.ds(128 * core, 128)] = dhalf2[...]

    def d_start(phase):
        for copy in d_copies(phase):
            copy.start()

    lax.fori_loop(0, LAG, send_out, 0)
    lax.fori_loop(0, 16, both, 0)
    dfull[...] = jnp.zeros_like(dfull)
    lax.fori_loop(0, blocks // 2, diagonal_local, 0)
    d_start(0)
    at = 16
    for phase in range(6):
        lax.fori_loop(at, at + 7, both, 0)
        at += 7
        d_arrive(phase)
        d_start(phase + 1)
    lax.fori_loop(at, 64, lambda k, c: take(k), 0)
    d_arrive(6)

    def slot(p, da, db, dc):
        digit = [0, 0, 0]
        digit[p], digit[(p + 1) % 3], digit[(p + 2) % 3] = da, db, dc
        return digit[0] * 16 + digit[1] * 4 + digit[2]

    for j in range(8):
        db = j // 2
        for p in range(3):
            for way in range(2):
                dc = j % 2 + 2 * way
                k = slot(p, 1 + way, db, dc)
                fwd_copy(1, p, way, k, j).wait_recv()
                acc[k, rows_of(p)] = acc[k, rows_of(p)] + fwd1[p][way, j]
                fin_copy(1, p, way, k, db * 4 + dc).start()
    for f in range(16):
        db, dc = f // 4, f % 4
        for p in range(3):
            k = slot(p, 3, db, dc)
            for way in range(2):
                fin_copy(1, p, way, k, f).wait_recv()
            acc[k, rows_of(p)] = acc[k, rows_of(p)] + fin1[p][0, f] + fin1[p][1, f]
            if db == 0:
                fwd_copy(2, p, dc // 2, k, dc % 2).start()
            if db == 1 and dc >= 2:
                fin_copy(2, p, 0, k, dc).start()
            if db == 2 and dc < 2:
                fin_copy(2, p, 1, k, dc).start()
    for j in range(2):
        for p in range(3):
            for way in range(2):
                dc = j + 2 * way
                k = slot(p, 3, 1 + way, dc)
                fwd_copy(2, p, way, k, j).wait_recv()
                acc[k, rows_of(p)] = acc[k, rows_of(p)] + fwd2[p][way, j]
                fin_copy(2, p, way, k, dc).start()

    def part3(p, way):
        low, size = ROWS[p]
        return (low, CUT) if way == 0 else (low + CUT, size - CUT)

    def fwd3_copy(p, way):
        low, size = part3(p, way)
        return remote(
            acc.at[slot(p, 3, 3, 0), pl.ds(low, size)], fwd3[p].at[way, pl.ds(0, size)],
            fwd3_send.at[p, way], fwd3_recv.at[p, way], peer((p + 2) % 3, (1, 3)[way]),
        )

    def fin3_copy(p, way, half):
        low, size = part3(p, half)
        return remote(
            acc.at[slot(p, 3, 3, 1 + way), pl.ds(low, size)],
            fin3[p].at[way, pl.ds(low - ROWS[p][0], size)],
            fin3_send.at[p, way, half], fin3_recv.at[p, way, half],
            peer((p + 2) % 3, (1, 3)[way]),
        )

    for dc in range(4):
        for p in range(3):
            k = slot(p, 3, 3, dc)
            for way in range(2):
                fin_copy(2, p, way, k, dc).wait_recv()
            acc[k, rows_of(p)] = acc[k, rows_of(p)] + fin2[p][0, dc] + fin2[p][1, dc]
            if dc == 0:
                fwd3_copy(p, 0).start()
                fwd3_copy(p, 1).start()
            if dc == 1:
                fin3_copy(p, 0, 1).start()
            if dc == 2:
                fin3_copy(p, 1, 0).start()
    for p in range(3):
        for way in range(2):
            low, size = part3(p, way)
            k = slot(p, 3, 3, 1 + way)
            fwd3_copy(p, way).wait_recv()
            acc[k, pl.ds(low, size)] = acc[k, pl.ds(low, size)] + fwd3[p][way, pl.ds(0, size)]
            fin3_copy(p, way, way).start()
    for p in range(3):
        for way in range(2):
            for half in range(2):
                fin3_copy(p, way, half).wait_recv()
        sum_ref[rows_of(p)] = acc[63, rows_of(p)] + fin3[p][0] + fin3[p][1]

    def drain_ring(k, carry):
        to_sibling(k).wait_send()
        return carry

    lax.fori_loop(64 - RING, 64, drain_ring, 0)
    for phase in range(7):
        for copy in d_copies(phase):
            copy.wait_send()

    def drain(i, carry):
        for p in range(3):
            for way in range(2):
                fin_copy(1, p, way, 0, i).wait_send()
        return carry

    def drain_half(i, carry):
        for p in range(3):
            for way in range(2):
                fwd_copy(1, p, way, 0, i).wait_send()
        return carry

    lax.fori_loop(0, 16, drain, 0)
    lax.fori_loop(0, 8, drain_half, 0)
    for p in range(3):
        for way in range(2):
            for j in range(2):
                fwd_copy(2, p, way, 0, j).wait_send()
                fin3_copy(p, way, j).wait_send()
            for j in range(4):
                fin_copy(2, p, way, 0, j).wait_send()
            fwd3_copy(p, way).wait_send()


def gather_and_sum(item, weight, strip_columns, tiles):
    blocks, width, rows = strip_columns.shape
    items = tiles.shape[0]
    dma = pltpu.SemaphoreType.DMA
    vmem = lambda *shape: pltpu.VMEM(shape, F32)
    sizes = [size for _, size in ROWS]
    any_space = pl.BlockSpec(memory_space=pl.ANY)
    in_vmem = pl.BlockSpec(memory_space=pltpu.VMEM)
    return pl.pallas_call(
        kernel,
        out_shape=[jax.ShapeDtypeStruct((256, 256), F32)] * 2,
        in_specs=[pl.BlockSpec(memory_space=pltpu.SMEM), in_vmem, any_space, any_space],
        out_specs=[in_vmem, in_vmem],
        scratch_shapes=[
            vmem(blocks, width, rows), vmem(items, width, rows),
            pltpu.VMEM((blocks + 1, rows, 4 * width), jnp.bfloat16),
            vmem(RING, 256, 256), vmem(64, 256, 256),
            *[vmem(2, 8, s, 256) for s in sizes], *[vmem(2, 16, s, 256) for s in sizes],
            *[vmem(2, 2, s, 256) for s in sizes], *[vmem(2, 4, s, 256) for s in sizes],
            *[vmem(2, CUT, 256) for s in sizes], *[vmem(2, s, 256) for s in sizes],
            vmem(256, 256), vmem(128, 256), vmem(128, 256), vmem(3, 32, 256), vmem(32, 256),
            vmem(3, 8, 256), vmem(4, 8, 256), vmem(32, 256), vmem(128, 256),
            dma((2,)), dma((64,)), dma((64,)),
            dma((3, 2, 8)), dma((3, 2, 8)), dma((3, 2, 16)), dma((3, 2, 16)),
            dma((3, 2, 2)), dma((3, 2, 2)), dma((3, 2, 4)), dma((3, 2, 4)),
            dma((3, 2)), dma((3, 2)), dma((3, 2, 2)), dma((3, 2, 2)),
            dma((7, 3)), dma((7, 3)),
        ],
        compiler_params=pltpu.CompilerParams(
            collective_id=0, has_side_effects=True, vmem_limit_bytes=60 << 20
        ),
    )(item, weight, strip_columns, tiles)


def per_device(strip_columns, tile_columns, barrier_weights, column_counts, tile_lists):
    highest = lax.Precision.HIGHEST
    blocks, width, rows = strip_columns.shape
    touched = tile_columns.shape[1]
    own_width = tile_columns.shape[3]
    devices = lax.axis_size(AXES)
    items = blocks * touched
    live_mask = jnp.arange(width, dtype=jnp.int32)[None, :] < column_counts[:, None]
    live_weight = jnp.where(live_mask, barrier_weights, 0.0)
    listed = tile_lists.reshape(1, items) == jnp.arange(devices, dtype=jnp.int32)[:, None]
    number = jnp.arange(items, dtype=jnp.int32)[None, :]
    least = jnp.min(jnp.where(listed, number, items), axis=1)
    most = jnp.max(jnp.where(listed, number, -1), axis=1)
    most = jnp.where((most == least) | (most < 0), items, most)
    slot = jnp.stack([least, most], axis=1).reshape(devices * 2)
    tile_sum, diagonal = gather_and_sum(
        slot,
        live_weight[:, :, None],
        strip_columns,
        tile_columns.reshape(items, width, own_width),
    )
    factor = jnp.linalg.cholesky(diagonal)
    inverse = jax.scipy.linalg.solve_triangular(
        factor, jnp.eye(rows, dtype=factor.dtype), lower=True
    )
    return (factor, jnp.dot(inverse, tile_sum, precision=highest))


def solution(mesh):
    return jax.shard_map(
        per_device,
        mesh=mesh,
        in_specs=(
            P(AXES, None, None),
            P(AXES, None, None, None),
            P(AXES, None),
            P(AXES),
            P(AXES, None),
        ),
        out_specs=(P(), P(None, AXES)),
        check_vma=False,
    )
```

```python
import functools

import jax
import jax.numpy as jnp
from jax import lax
from jax.experimental import pallas as pl
from jax.experimental.pallas import tpu as pltpu
from jax.sharding import PartitionSpec as P

AXES = ("row", "col")
MESH = pl.DeviceIdType.MESH
ROWS = ((0, 88), (88, 88), (176, 80))
CUT = 48
PACE = 5
SECOND = (88, 92, 100, 106, 112, 118, 126)
STRIDE = (16, 4, 1)
LAG = 2
RING = 16
OFFSET = (2, 1, 3, 0)
F32 = jnp.float32


def split(x):
    high = x.astype(jnp.bfloat16)
    return high, (x - high.astype(F32)).astype(jnp.bfloat16)


def dot(a, b):
    return lax.dot_general(a, b, (((1,), (0,)), ((), ())), preferred_element_type=F32)


def full_dot(a, b, turned=False):
    return lax.dot_general(
        a, b, (((1,), (1 if turned else 0,)), ((), ())),
        precision=lax.Precision.HIGHEST, preferred_element_type=F32,
    )


def diagonal_of(r):
    i = lax.broadcasted_iota(jnp.int32, (r, r), 0)
    return i, lax.broadcasted_iota(jnp.int32, (r, r), 1)


def open_block(a):
    i, j = diagonal_of(128)
    both = jnp.concatenate([a, jnp.where(i == j, 1.0, 0.0)], axis=1)
    return [both[8 * g : 8 * g + 8] for g in range(16)]


def eliminate(groups):
    below = lax.broadcasted_iota(jnp.int32, (8, 1), 0)
    for k in range(0, 128, 2):
        top, s = k // 8, k % 8
        one, two = groups[top][s : s + 1], groups[top][s + 1 : s + 2]
        a, b, c = one[:, k : k + 1], one[:, k + 1 : k + 2], two[:, k + 1 : k + 2]
        first = 1.0 / a
        second = a / (a * c - b * b)
        ratio = b * first
        scaled_one, scaled_two = one * first, (two - ratio * one) * second
        for g in range(top, 16):
            left = groups[g][:, k : k + 1]
            right = groups[g][:, k + 1 : k + 2] - ratio * left
            if g == top:
                left = jnp.where(below > s, left, 0.0)
                right = jnp.where(below > s + 1, right, 0.0)
            groups[g] = groups[g] - left * scaled_one - right * scaled_two
        yield


def close_block(groups):
    both = jnp.concatenate(groups, axis=0)
    i, j = diagonal_of(128)
    pivots = jnp.sum(jnp.where(i == j, both[:, :128], 0.0), axis=1, keepdims=True)
    both = both * (1.0 / jnp.sqrt(pivots))
    return jnp.where(j >= i, both[:, :128], 0.0).T, both[:, 128:]


def factorize(d_ref, l_ref, inverse_ref):
    groups = open_block(d_ref[:128, :128])
    yield from eliminate(groups)
    upper, upper_inverse = close_block(groups)
    between = full_dot(d_ref[128:, :128], upper_inverse, True)
    zero = jnp.zeros((128, 128), F32)
    l_ref[:128, :128] = upper
    l_ref[:128, 128:] = zero
    l_ref[128:, :128] = between
    inverse_ref[:128, :128] = upper_inverse
    inverse_ref[:128, 128:] = zero
    groups = open_block(d_ref[128:, 128:] - full_dot(between, between, True))
    yield from eliminate(groups)
    lower, lower_inverse = close_block(groups)
    l_ref[128:, 128:] = lower
    inverse_ref[128:, 128:] = lower_inverse
    inverse_ref[128:, :128] = -full_dot(
        lower_inverse, full_dot(l_ref[128:, :128], inverse_ref[:128, :128])
    )


def kernel(
    item_ref, weight_ref, strip_ref, tile_ref, factor_ref, update_ref,
    strip, tile, left, sent, acc,
    fwd10, fwd11, fwd12, fin10, fin11, fin12,
    fwd20, fwd21, fwd22, fin20, fin21, fin22,
    fwd30, fwd31, fwd32, fin30, fin31, fin32,
    inverse_ref, total, diagonal_ref, dfull, dpair, dhalf, dx, dquarter, dy, dz, dquarter2, dhalf2,
    load_sem, sib_send, sib_recv,
    fwd1_send, fwd1_recv, fin1_send, fin1_recv,
    fwd2_send, fwd2_recv, fin2_send, fin2_recv,
    fwd3_send, fwd3_recv, fin3_send, fin3_recv,
    d_send, d_recv,
):
    fwd1, fin1 = (fwd10, fwd11, fwd12), (fin10, fin11, fin12)
    fwd2, fin2 = (fwd20, fwd21, fwd22), (fin20, fin21, fin22)
    fwd3, fin3 = (fwd30, fwd31, fwd32), (fin30, fin31, fin32)
    row, col = lax.axis_index("row"), lax.axis_index("col")
    core = lax.rem(row, 2)
    place = (lax.div(row, 2), lax.div(col, 4), lax.rem(col, 4))
    blocks = strip.shape[0]

    def device(y, x, z, c):
        return (y * 2 + c, x * 4 + z)

    def peer(axis, step):
        at = list(place)
        at[axis] = lax.rem(at[axis] + step, 4)
        return device(*at, core)

    sibling = device(*place, 1 - core)

    barrier = pltpu.get_barrier_semaphore()
    partners = [peer(a, s) for a in range(3) for s in (1, 2, 3)] + [sibling]
    for partner in partners:
        pl.semaphore_signal(barrier, inc=1, device_id=partner, device_id_type=MESH)
    get_strip = pltpu.make_async_copy(strip_ref, strip, load_sem.at[0])
    get_tile = pltpu.make_async_copy(tile_ref, tile, load_sem.at[1])
    get_strip.start()
    get_tile.start()
    get_strip.wait()

    left[blocks] = jnp.zeros(left.shape[1:], left.dtype)

    def build(b, carry):
        scaled = strip[b] * weight_ref[b]
        high = scaled.astype(jnp.bfloat16).astype(F32)
        low = scaled - high
        stack = jnp.concatenate([high, high, low, low], axis=0)
        left[b] = stack.T.astype(jnp.bfloat16)
        return carry

    lax.fori_loop(0, blocks, build, 0)
    get_tile.wait()
    pl.semaphore_wait(barrier, len(partners))

    def remote(src, dst, send, recv, to):
        return pltpu.make_async_remote_copy(
            src_ref=src, dst_ref=dst, send_sem=send, recv_sem=recv,
            device_id=to, device_id_type=MESH,
        )

    def product(ty, tx, tz, c):
        number = ((ty * 2 + c) * 4 + tx) * 4 + tz
        lefts, rights = [], []
        for n in range(2):
            slot = item_ref[2 * number + n]
            lefts.append(left[lax.div(slot, 4)])
            high, low = split(tile[lax.rem(slot, tile.shape[0])])
            rights += [high, low, high, low]
        return dot(jnp.concatenate(lefts, axis=1), jnp.concatenate(rights, axis=0))

    def offset(d):
        return jnp.where(d == 0, 2, jnp.where(d == 1, 1, jnp.where(d == 2, 3, 0)))

    def group_tiles(i, c):
        ty = lax.rem(place[0] + offset(lax.div(i, 4)), 4)
        tx = lax.rem(place[1] + offset(lax.rem(i, 4)), 4)
        return [functools.partial(product, ty, tx, lax.rem(place[2] + o, 4), c) for o in OFFSET]

    def to_sibling(k):
        return remote(
            sent.at[lax.rem(k, RING)], acc.at[k], sib_send.at[k], sib_recv.at[k], sibling
        )

    def rows_of(p):
        return pl.ds(*ROWS[p])

    def fwd_copy(stage, p, way, k, j):
        fwd = (fwd1, fwd2)[stage - 1]
        send, recv = ((fwd1_send, fwd1_recv), (fwd2_send, fwd2_recv))[stage - 1]
        axis = (p + stage - 1) % 3
        return remote(
            acc.at[k, rows_of(p)], fwd[p].at[way, j],
            send.at[p, way, j], recv.at[p, way, j], peer(axis, 1 + 2 * way),
        )

    def fin_copy(stage, p, way, k, j):
        fin = (fin1, fin2)[stage - 1]
        send, recv = ((fin1_send, fin1_recv), (fin2_send, fin2_recv))[stage - 1]
        axis = (p + stage - 1) % 3
        return remote(
            acc.at[k, rows_of(p)], fin[p].at[way, j],
            send.at[p, way, j], recv.at[p, way, j], peer(axis, 1 + 2 * way),
        )

    def send_on(i, dz):
        k = 4 * i + dz
        digit = (lax.div(i, 4), lax.rem(i, 4), dz)
        for p in range(3):
            da, db, dc = digit[p], digit[(p + 1) % 3], digit[(p + 2) % 3]
            if p == 2 and dz == 3:
                continue

            if p != 2 or dz == 0:
                @pl.when(da == 0)
                def _():
                    way = jnp.where(dc < 2, 0, 1)
                    fwd_copy(1, p, way, k, db * 2 + lax.rem(dc, 2)).start()

            if p != 2 or dz > 0:
                @pl.when(((da == 1) & (dc >= 2)) | ((da == 2) & (dc < 2)))
                def _():
                    fin_copy(1, p, da - 1, k, db * 4 + dc).start()

    def give_group(i, fresh=False):
        for n, term in enumerate(group_tiles(i, 1 - core)):
            sent[lax.rem(4 * i + n, RING)] = term()

    def give(i, carry):
        give_group(i)
        for n in range(4):
            to_sibling(4 * i + n).start()
        return carry

    def take_group(i):
        for n, term in enumerate(group_tiles(i, core)):
            acc[4 * i + n] = acc[4 * i + n] + term()

    def take(i, carry):
        for n in range(4):
            to_sibling(4 * i + n).wait_recv()
        take_group(i)
        for n in range(4):
            send_on(i, n)
        return carry

    def both(i, carry):
        @pl.when(i >= RING // 4 - LAG)
        def _():
            for n in range(4):
                to_sibling(4 * (i + LAG) - RING + n).wait_send()

        for n in range(4):
            to_sibling(4 * i + n).wait_recv()
        give_group(i + LAG)
        take_group(i)
        for n in range(4):
            to_sibling(4 * (i + LAG) + n).start()
        for n in range(4):
            send_on(i, n)

        @pl.when(i == 3)
        def _():
            dfull[...] = jnp.zeros_like(dfull)
            lax.fori_loop(0, blocks // 2, diagonal_local, 0)
            d_start(0)

        for phase, after in enumerate((5, 7, 9, 11, 13)):
            @pl.when(i == after)
            def _():
                d_arrive(phase)
                d_start(phase + 1)

        return carry

    def diagonal_local(b, carry):
        lefts, rights = [], []
        for s in range(2):
            lefts.append(left[2 * b + s])
            high, low = split(strip[2 * b + s])
            rights += [high, low, high, low]
        dfull[...] = dfull[...] + dot(
            jnp.concatenate(lefts, axis=1), jnp.concatenate(rights, axis=0)
        )
        return carry

    def d_copies(phase):
        py, px, pz = place
        if phase == 0:
            return [remote(dfull.at[pl.ds(128 * (1 - core), 128)], dpair, d_send.at[0, 0], d_recv.at[0, 0], sibling)]
        if phase == 6:
            return [remote(dhalf2, diagonal_ref.at[pl.ds(128 * core, 128)], d_send.at[6, 0], d_recv.at[6, 0], sibling)]
        out = []
        for o in (1, 2, 3):
            if phase == 1:
                src, dst, axis = dhalf.at[pl.ds(32 * lax.rem(px + o, 4), 32)], dx.at[o - 1], 1
            elif phase == 2:
                src, dst, axis = dquarter.at[pl.ds(8 * lax.rem(py + o, 4), 8)], dy.at[o - 1], 0
            elif phase == 3:
                src, dst, axis = dz.at[pz], dz.at[pz], 2
            elif phase == 4:
                part = pl.ds(8 * py, 8)
                src, dst, axis = dquarter2.at[part], dquarter2.at[part], 0
            else:
                part = pl.ds(32 * px, 32)
                src, dst, axis = dhalf2.at[part], dhalf2.at[part], 1
            out.append(remote(src, dst, d_send.at[phase, o - 1], d_recv.at[phase, o - 1], peer(axis, o)))
        return out

    def d_arrive(phase):
        py, px, pz = place
        for o, copy in enumerate(d_copies(phase)):
            copy.wait_recv()
        if phase == 0:
            dhalf[...] = dfull[pl.ds(128 * core, 128)] + dpair[...]
        elif phase == 1:
            dquarter[...] = dhalf[pl.ds(32 * px, 32)] + dx[0] + dx[1] + dx[2]
        elif phase == 2:
            dz[pz] = dquarter[pl.ds(8 * py, 8)] + dy[0] + dy[1] + dy[2]
        elif phase == 3:
            dquarter2[pl.ds(8 * py, 8)] = dz[0] + dz[1] + dz[2] + dz[3]
        elif phase == 4:
            dhalf2[pl.ds(32 * px, 32)] = dquarter2[...]
        elif phase == 5:
            diagonal_ref[pl.ds(128 * core, 128)] = dhalf2[...]

    def d_start(phase):
        for copy in d_copies(phase):
            copy.start()

    lax.fori_loop(0, LAG, give, 0)
    lax.fori_loop(0, 16 - LAG, both, 0)
    lax.fori_loop(16 - LAG, 16, take, 0)
    d_arrive(5)
    d_start(6)

    def slot(p, da, db, dc):
        digit = [0, 0, 0]
        digit[p], digit[(p + 1) % 3], digit[(p + 2) % 3] = da, db, dc
        return digit[0] * 16 + digit[1] * 4 + digit[2]

    for j in range(8):
        db = j // 2
        for p in range(3):
            for way in range(2):
                dc = j % 2 + 2 * way
                k = slot(p, 1 + way, db, dc)
                fwd_copy(1, p, way, k, j).wait_recv()
                acc[k, rows_of(p)] = acc[k, rows_of(p)] + fwd1[p][way, j]
                fin_copy(1, p, way, k, db * 4 + dc).start()
    def gather1(f):
        db, dc = f // 4, f % 4
        for p in range(3):
            k = slot(p, 3, db, dc)
            for way in range(2):
                fin_copy(1, p, way, k, f).wait_recv()
            acc[k, rows_of(p)] = acc[k, rows_of(p)] + fin1[p][0, f] + fin1[p][1, f]
            if db == 0:
                fwd_copy(2, p, dc // 2, k, dc % 2).start()
            if db == 1 and dc >= 2:
                fin_copy(2, p, 0, k, dc).start()
            if db == 2 and dc < 2:
                fin_copy(2, p, 1, k, dc).start()
    def pass2(j):
        for p in range(3):
            for way in range(2):
                dc = j + 2 * way
                k = slot(p, 3, 1 + way, dc)
                fwd_copy(2, p, way, k, j).wait_recv()
                acc[k, rows_of(p)] = acc[k, rows_of(p)] + fwd2[p][way, j]
                fin_copy(2, p, way, k, dc).start()

    def part3(p, way):
        low, size = ROWS[p]
        return (low, CUT) if way == 0 else (low + CUT, size - CUT)

    def fwd3_copy(p, way):
        low, size = part3(p, way)
        return remote(
            acc.at[slot(p, 3, 3, 0), pl.ds(low, size)], fwd3[p].at[way, pl.ds(0, size)],
            fwd3_send.at[p, way], fwd3_recv.at[p, way], peer((p + 2) % 3, (1, 3)[way]),
        )

    def fin3_copy(p, way, half):
        low, size = part3(p, half)
        return remote(
            acc.at[slot(p, 3, 3, 1 + way), pl.ds(low, size)],
            fin3[p].at[way, pl.ds(low - ROWS[p][0], size)],
            fin3_send.at[p, way, half], fin3_recv.at[p, way, half],
            peer((p + 2) % 3, (1, 3)[way]),
        )

    def gather2(dc):
        for p in range(3):
            k = slot(p, 3, 3, dc)
            for way in range(2):
                fin_copy(2, p, way, k, dc).wait_recv()
            acc[k, rows_of(p)] = acc[k, rows_of(p)] + fin2[p][0, dc] + fin2[p][1, dc]
            if dc == 0:
                fwd3_copy(p, 0).start()
                fwd3_copy(p, 1).start()
            if dc == 1:
                fin3_copy(p, 0, 1).start()
            if dc == 2:
                fin3_copy(p, 1, 0).start()
    def pass3():
        for p in range(3):
            for way in range(2):
                low, size = part3(p, way)
                k = slot(p, 3, 3, 1 + way)
                fwd3_copy(p, way).wait_recv()
                acc[k, pl.ds(low, size)] = acc[k, pl.ds(low, size)] + fwd3[p][way, pl.ds(0, size)]
                fin3_copy(p, way, way).start()

    def gather3():
        for p in range(3):
            for way in range(2):
                for half in range(2):
                    fin3_copy(p, way, half).wait_recv()
            total[rows_of(p)] = acc[63, rows_of(p)] + fin3[p][0] + fin3[p][1]

    d_arrive(6)
    moves = {PACE * (f + 1): functools.partial(gather1, f) for f in range(16)}
    moves |= {SECOND[j]: functools.partial(pass2, j) for j in range(2)}
    moves |= {SECOND[2 + dc]: functools.partial(gather2, dc) for dc in range(4)}
    moves[SECOND[6]] = pass3
    step = 0
    for _ in factorize(diagonal_ref, factor_ref, inverse_ref):
        step += 1
        if step in moves:
            moves.pop(step)()
    for step in sorted(moves):
        moves[step]()
    gather3()
    update_ref[...] = full_dot(inverse_ref[...], total[...])

    def drain_ring(k, carry):
        to_sibling(k).wait_send()
        return carry

    lax.fori_loop(64 - RING, 64, drain_ring, 0)
    for phase in range(7):
        for copy in d_copies(phase):
            copy.wait_send()

    def drain(i, carry):
        for p in range(3):
            for way in range(2):
                fin_copy(1, p, way, 0, i).wait_send()
        return carry

    def drain_half(i, carry):
        for p in range(3):
            for way in range(2):
                fwd_copy(1, p, way, 0, i).wait_send()
        return carry

    lax.fori_loop(0, 16, drain, 0)
    lax.fori_loop(0, 8, drain_half, 0)
    for p in range(3):
        for way in range(2):
            for j in range(2):
                fwd_copy(2, p, way, 0, j).wait_send()
                fin3_copy(p, way, j).wait_send()
            for j in range(4):
                fin_copy(2, p, way, 0, j).wait_send()
            fwd3_copy(p, way).wait_send()


def gather_and_sum(item, weight, strip_columns, tiles):
    blocks, width, rows = strip_columns.shape
    items = tiles.shape[0]
    dma = pltpu.SemaphoreType.DMA
    vmem = lambda *shape: pltpu.VMEM(shape, F32)
    sizes = [size for _, size in ROWS]
    any_space = pl.BlockSpec(memory_space=pl.ANY)
    in_vmem = pl.BlockSpec(memory_space=pltpu.VMEM)
    return pl.pallas_call(
        kernel,
        out_shape=[jax.ShapeDtypeStruct((256, 256), F32)] * 2,
        in_specs=[pl.BlockSpec(memory_space=pltpu.SMEM), in_vmem, any_space, any_space],
        out_specs=[in_vmem, in_vmem],
        scratch_shapes=[
            vmem(blocks, width, rows), vmem(items, width, rows),
            pltpu.VMEM((blocks + 1, rows, 4 * width), jnp.bfloat16),
            vmem(RING, 256, 256), vmem(64, 256, 256),
            *[vmem(2, 8, s, 256) for s in sizes], *[vmem(2, 16, s, 256) for s in sizes],
            *[vmem(2, 2, s, 256) for s in sizes], *[vmem(2, 4, s, 256) for s in sizes],
            *[vmem(2, CUT, 256) for s in sizes], *[vmem(2, s, 256) for s in sizes],
            vmem(256, 256), vmem(256, 256), vmem(256, 256),
            vmem(256, 256), vmem(128, 256), vmem(128, 256), vmem(3, 32, 256), vmem(32, 256),
            vmem(3, 8, 256), vmem(4, 8, 256), vmem(32, 256), vmem(128, 256),
            dma((2,)), dma((64,)), dma((64,)),
            dma((3, 2, 8)), dma((3, 2, 8)), dma((3, 2, 16)), dma((3, 2, 16)),
            dma((3, 2, 2)), dma((3, 2, 2)), dma((3, 2, 4)), dma((3, 2, 4)),
            dma((3, 2)), dma((3, 2)), dma((3, 2, 2)), dma((3, 2, 2)),
            dma((7, 3)), dma((7, 3)),
        ],
        compiler_params=pltpu.CompilerParams(
            collective_id=0, has_side_effects=True, vmem_limit_bytes=60 << 20
        ),
    )(item, weight, strip_columns, tiles)


def per_device(strip_columns, tile_columns, barrier_weights, column_counts, tile_lists):
    blocks, width, rows = strip_columns.shape
    touched = tile_columns.shape[1]
    own_width = tile_columns.shape[3]
    devices = lax.axis_size(AXES)
    items = blocks * touched
    live_mask = jnp.arange(width, dtype=jnp.int32)[None, :] < column_counts[:, None]
    live_weight = jnp.where(live_mask, barrier_weights, 0.0)
    listed = tile_lists.reshape(1, items) == jnp.arange(devices, dtype=jnp.int32)[:, None]
    number = jnp.arange(items, dtype=jnp.int32)[None, :]
    least = jnp.min(jnp.where(listed, number, items), axis=1)
    most = jnp.max(jnp.where(listed, number, -1), axis=1)
    most = jnp.where((most == least) | (most < 0), items, most)
    slot = jnp.stack([least, most], axis=1).reshape(devices * 2)
    return gather_and_sum(
        slot,
        live_weight[:, :, None],
        strip_columns,
        tile_columns.reshape(items, width, own_width),
    )


def solution(mesh):
    return jax.shard_map(
        per_device,
        mesh=mesh,
        in_specs=(
            P(AXES, None, None),
            P(AXES, None, None, None),
            P(AXES, None),
            P(AXES),
            P(AXES, None),
        ),
        out_specs=(P(), P(None, AXES)),
        check_vma=False,
    )
```

```python
import functools

import jax
import jax.numpy as jnp
from jax import lax
from jax.experimental import pallas as pl
from jax.experimental.pallas import tpu as pltpu
from jax.sharding import PartitionSpec as P

AXES = ("row", "col")
MESH = pl.DeviceIdType.MESH
ROWS = ((0, 88), (88, 88), (176, 80))
CUT = 48
TURNS = (1, 4, 8)
PACE = 5
SECOND = (88, 92, 100, 106, 112, 118, 126)
STRIDE = (16, 4, 1)
F32 = jnp.float32


def split(x):
    high = x.astype(jnp.bfloat16)
    return high, (x - high.astype(F32)).astype(jnp.bfloat16)


def dot(a, b):
    return lax.dot_general(a, b, (((1,), (0,)), ((), ())), preferred_element_type=F32)


def full_dot(a, b, turned=False):
    return lax.dot_general(
        a, b, (((1,), (1 if turned else 0,)), ((), ())),
        precision=lax.Precision.HIGHEST, preferred_element_type=F32,
    )


def diagonal_of(r):
    i = lax.broadcasted_iota(jnp.int32, (r, r), 0)
    return i, lax.broadcasted_iota(jnp.int32, (r, r), 1)


def open_block(a):
    i, j = diagonal_of(128)
    both = jnp.concatenate([a, jnp.where(i == j, 1.0, 0.0)], axis=1)
    return [both[8 * g : 8 * g + 8] for g in range(16)]


def eliminate(groups):
    below = lax.broadcasted_iota(jnp.int32, (8, 1), 0)
    for k in range(0, 128, 2):
        top, s = k // 8, k % 8
        one, two = groups[top][s : s + 1], groups[top][s + 1 : s + 2]
        a, b, c = one[:, k : k + 1], one[:, k + 1 : k + 2], two[:, k + 1 : k + 2]
        first = 1.0 / a
        second = a / (a * c - b * b)
        ratio = b * first
        scaled_one, scaled_two = one * first, (two - ratio * one) * second
        for g in range(top, 16):
            left = groups[g][:, k : k + 1]
            right = groups[g][:, k + 1 : k + 2] - ratio * left
            if g == top:
                left = jnp.where(below > s, left, 0.0)
                right = jnp.where(below > s + 1, right, 0.0)
            groups[g] = groups[g] - left * scaled_one - right * scaled_two
        yield


def close_block(groups):
    both = jnp.concatenate(groups, axis=0)
    i, j = diagonal_of(128)
    pivots = jnp.sum(jnp.where(i == j, both[:, :128], 0.0), axis=1, keepdims=True)
    both = both * (1.0 / jnp.sqrt(pivots))
    return jnp.where(j >= i, both[:, :128], 0.0).T, both[:, 128:]


def factorize(d_ref, l_ref, inverse_ref):
    groups = open_block(d_ref[:128, :128])
    yield from eliminate(groups)
    upper, upper_inverse = close_block(groups)
    between = full_dot(d_ref[128:, :128], upper_inverse, True)
    zero = jnp.zeros((128, 128), F32)
    l_ref[:128, :128] = upper
    l_ref[:128, 128:] = zero
    l_ref[128:, :128] = between
    inverse_ref[:128, :128] = upper_inverse
    inverse_ref[:128, 128:] = zero
    groups = open_block(d_ref[128:, 128:] - full_dot(between, between, True))
    yield from eliminate(groups)
    lower, lower_inverse = close_block(groups)
    l_ref[128:, 128:] = lower
    inverse_ref[128:, 128:] = lower_inverse
    inverse_ref[128:, :128] = -full_dot(
        lower_inverse, full_dot(l_ref[128:, :128], inverse_ref[:128, :128])
    )


def kernel(
    weight_ref, count_ref, list_ref, strip_ref, tile_ref, factor_ref, update_ref,
    strip, scaled, tile, left, lives, slots, table, acc,
    fwd10, fwd11, fwd12, fin10, fin11, fin12,
    fwd20, fwd21, fwd22, fin20, fin21, fin22,
    fwd30, fwd31, fwd32, fin30, fin31, fin32,
    inverse_ref, total, diagonal_ref, dfull, dx, dquarter, dy, dz, dquarter2,
    load_sem, sib_send, sib_recv,
    fwd1_send, fwd1_recv, fin1_send, fin1_recv,
    fwd2_send, fwd2_recv, fin2_send, fin2_recv,
    fwd3_send, fwd3_recv, fin3_send, fin3_recv,
    d_send, d_recv,
):
    fwd1, fin1 = (fwd10, fwd11, fwd12), (fin10, fin11, fin12)
    fwd2, fin2 = (fwd20, fwd21, fwd22), (fin20, fin21, fin22)
    fwd3, fin3 = (fwd30, fwd31, fwd32), (fin30, fin31, fin32)
    row, col = lax.axis_index("row"), lax.axis_index("col")
    core = lax.rem(row, 2)
    place = (lax.div(row, 2), lax.div(col, 4), lax.rem(col, 4))
    blocks, items, width = strip_ref.shape[0], tile_ref.shape[0], strip_ref.shape[1]

    def device(y, x, z, c):
        return (y * 2 + c, x * 4 + z)

    def peer(axis, step):
        at = list(place)
        at[axis] = lax.rem(at[axis] + step, 4)
        return device(*at, core)

    sibling = device(*place, 1 - core)

    def plane_peer(step, flip):
        return device(
            place[0], lax.rem(place[1] + step, 4), place[2], 1 - core if flip else core
        )

    around = [(step, flip) for step in range(4) for flip in (0, 1) if step or flip]

    barrier = pltpu.get_barrier_semaphore()
    partners = [peer(a, s) for a in (0, 2) for s in (1, 2, 3)] + [plane_peer(*at) for at in around]
    for partner in partners:
        pl.semaphore_signal(barrier, inc=1, device_id=partner, device_id_type=MESH)
    get_strip = pltpu.make_async_copy(strip_ref, strip.at[pl.ds(0, blocks)], load_sem.at[0])
    get_tile = pltpu.make_async_copy(tile_ref, tile.at[pl.ds(0, items)], load_sem.at[1])
    get_strip.start()
    get_tile.start()

    lane = lax.broadcasted_iota(jnp.int32, (blocks, 128), 1)
    block = lax.broadcasted_iota(jnp.int32, (blocks, 128), 0)
    least = jnp.full((blocks, 128), items, jnp.int32)
    most = jnp.full((blocks, 128), -1, jnp.int32)
    for k in range(4):
        listed = list_ref[:, k : k + 1] == lane
        number = block * 4 + k
        least = jnp.minimum(least, jnp.where(listed, number, items))
        most = jnp.maximum(most, jnp.where(listed, number, -1))
    least = jnp.min(least, axis=0, keepdims=True)
    most = jnp.max(most, axis=0, keepdims=True)
    slots[0, 0:1] = least
    slots[0, 1:2] = jnp.where((most == least) | (most < 0), items, most)
    own_table = pltpu.make_async_copy(slots.at[0], table.at[0], load_sem.at[2])
    own_table.start()

    column = lax.broadcasted_iota(jnp.int32, (width, blocks), 0)
    lives[0] = jnp.zeros(lives.shape[1:], F32)
    lives[0, :, :blocks] = jnp.where(column < count_ref[...], weight_ref[...].T, 0.0)
    pl.semaphore_wait(barrier, len(partners))

    def remote(src, dst, send, recv, to):
        return pltpu.make_async_remote_copy(
            src_ref=src, dst_ref=dst, send_sem=send, recv_sem=recv,
            device_id=to, device_id_type=MESH,
        )

    def build(first, skip):
        def body(q, carry):
            for n in range(4):
                b = first + 4 * q + n
                high = scaled[b].astype(jnp.bfloat16).astype(F32)
                low = scaled[b] - high
                stack = jnp.concatenate([high, high, low, low], axis=0)
                left[b + skip] = stack.T.astype(jnp.bfloat16)
            return carry

        lax.fori_loop(0, blocks // 4, body, 0)

    def weigh(n):
        live = lives[n]
        for b in range(blocks):
            scaled[n * blocks + b] = strip[n * blocks + b] * live[:, b : b + 1]

    across = [
        remote(src, dst, sib_send.at[n], sib_recv.at[n], sibling)
        for n, (src, dst) in enumerate([
            (lives.at[0], lives.at[1]),
            (strip_ref, strip.at[pl.ds(blocks, blocks)]),
            (slots.at[0], slots.at[1]),
            (tile_ref, tile.at[pl.ds(items, items)]),
        ])
    ]
    for copy in across:
        copy.start()
    zero = jnp.zeros(left.shape[1:], left.dtype)
    left[blocks] = zero
    left[2 * blocks + 1] = zero
    get_strip.wait()
    weigh(0)
    build(0, 0)

    def product(ty, tx, tz):
        number = ((ty * 2 + core) * 4 + tx) * 4 + tz
        lefts, rights = [], []
        for n in range(4):
            slot = table[n // 2, n % 2, number]
            lefts.append(left[lax.div(slot, 4) + (n // 2) * (blocks + 1)])
            high, low = split(tile[lax.rem(slot, items) + (n // 2) * items])
            rights += [high, low, high, low]
        return dot(jnp.concatenate(lefts, axis=1), jnp.concatenate(rights, axis=0))

    def offset(d):
        return jnp.where(d == 0, 2, jnp.where(d == 1, 1, jnp.where(d == 2, 3, 0)))

    def group_digits(i):
        turn, at = lax.div(i, 4), lax.rem(i, 4)
        y = jnp.where(at == 0, 0, jnp.where(at == 1, 3, at - 1))
        return [(y, x, lax.rem(turn + 8 - y - x, 4)) for x in range(4)]

    def rows_of(p):
        return pl.ds(*ROWS[p])

    def fwd_copy(stage, p, way, k, j):
        fwd = (fwd1, fwd2)[stage - 1]
        send, recv = ((fwd1_send, fwd1_recv), (fwd2_send, fwd2_recv))[stage - 1]
        axis = (p + stage - 1) % 3
        return remote(
            acc.at[k, rows_of(p)], fwd[p].at[way, j],
            send.at[p, way, j], recv.at[p, way, j], peer(axis, 1 + 2 * way),
        )

    def fin_copy(stage, p, way, k, j):
        fin = (fin1, fin2)[stage - 1]
        send, recv = ((fin1_send, fin1_recv), (fin2_send, fin2_recv))[stage - 1]
        axis = (p + stage - 1) % 3
        return remote(
            acc.at[k, rows_of(p)], fin[p].at[way, j],
            send.at[p, way, j], recv.at[p, way, j], peer(axis, 1 + 2 * way),
        )

    def send_on(k, digit):
        for p in range(3):
            da, db, dc = digit[p], digit[(p + 1) % 3], digit[(p + 2) % 3]

            if isinstance(da, int):
                da = jnp.int32(da)

            @pl.when(da == 0)
            def _():
                way = jnp.where(dc < 2, 0, 1)
                fwd_copy(1, p, way, k, db * 2 + lax.rem(dc, 2)).start()

            @pl.when(((da == 1) & (dc >= 2)) | ((da == 2) & (dc < 2)))
            def _():
                fin_copy(1, p, da - 1, k, db * 4 + dc).start()

    def tiles(i, carry):
        group = group_digits(i)
        at = [y * 16 + x * 4 + z for y, x, z in group]
        for k, digit in zip(at, group):
            acc[k] = product(*[lax.rem(place[a] + offset(digit[a]), 4) for a in range(3)])
        for k, digit in zip(at, group):
            send_on(k, digit)
        for phase, after in enumerate(TURNS):
            @pl.when(i == after)
            def _():
                d_arrive(phase + 1)
                d_start(phase + 2)

        return carry

    def diagonal_local(b, carry):
        lefts, rights = [], []
        for n in range(2):
            lefts.append(left[2 * b + n])
            high, low = split(strip[2 * b + n])
            rights += [high, low, high, low]
        dfull[...] = dfull[...] + dot(
            jnp.concatenate(lefts, axis=1), jnp.concatenate(rights, axis=0)
        )
        return carry

    py, px, pz = place
    mine = pl.ds(pl.multiple_of(64 * px + 32 * core, 32), 32)

    def d_copies(phase):
        out = []
        if phase in (0, 4):
            for n, (step, flip) in enumerate(around):
                there = 2 * lax.rem(px + step, 4) + (1 - core if flip else core)
                if phase == 0:
                    src, dst = dfull.at[pl.ds(pl.multiple_of(32 * there, 32), 32)], dx.at[n]
                else:
                    src = dst = diagonal_ref.at[mine]
                out.append(remote(src, dst, d_send.at[phase, n], d_recv.at[phase, n], plane_peer(step, flip)))
            return out
        for o in (1, 2, 3):
            if phase == 1:
                src, dst, axis = dquarter.at[pl.ds(8 * lax.rem(py + o, 4), 8)], dy.at[o - 1], 0
            elif phase == 2:
                src, dst, axis = dz.at[pz], dz.at[pz], 2
            else:
                part = pl.ds(8 * py, 8)
                src, dst, axis = dquarter2.at[part], dquarter2.at[part], 0
            out.append(remote(src, dst, d_send.at[phase, o - 1], d_recv.at[phase, o - 1], peer(axis, o)))
        return out

    def d_arrive(phase):
        for copy in d_copies(phase):
            copy.wait_recv()
        if phase == 0:
            held = dfull[mine]
            for n in range(len(around)):
                held = held + dx[n]
            dquarter[...] = held
        elif phase == 1:
            dz[pz] = dquarter[pl.ds(8 * py, 8)] + dy[0] + dy[1] + dy[2]
        elif phase == 2:
            dquarter2[pl.ds(8 * py, 8)] = dz[0] + dz[1] + dz[2] + dz[3]
        elif phase == 3:
            diagonal_ref[mine] = dquarter2[...]

    def d_start(phase):
        for copy in d_copies(phase):
            copy.start()

    dfull[...] = jnp.zeros_like(dfull)
    lax.fori_loop(0, blocks // 2, diagonal_local, 0)
    d_start(0)
    across[0].wait_recv()
    across[1].wait_recv()
    weigh(1)
    build(blocks, 1)
    across[2].wait_recv()
    their_table = pltpu.make_async_copy(slots.at[1], table.at[1], load_sem.at[3])
    their_table.start()
    d_arrive(0)
    d_start(1)
    own_table.wait()
    their_table.wait()
    get_tile.wait()
    across[3].wait_recv()
    lax.fori_loop(0, 16, tiles, 0)

    def slot(p, da, db, dc):
        digit = [0, 0, 0]
        digit[p], digit[(p + 1) % 3], digit[(p + 2) % 3] = da, db, dc
        return digit[0] * 16 + digit[1] * 4 + digit[2]

    for j in range(8):
        db = j // 2
        for p in range(3):
            for way in range(2):
                dc = j % 2 + 2 * way
                k = slot(p, 1 + way, db, dc)
                fwd_copy(1, p, way, k, j).wait_recv()
                acc[k, rows_of(p)] = acc[k, rows_of(p)] + fwd1[p][way, j]
                fin_copy(1, p, way, k, db * 4 + dc).start()
    def gather1(f):
        db, dc = f // 4, f % 4
        for p in range(3):
            k = slot(p, 3, db, dc)
            for way in range(2):
                fin_copy(1, p, way, k, f).wait_recv()
            acc[k, rows_of(p)] = acc[k, rows_of(p)] + fin1[p][0, f] + fin1[p][1, f]
            if db == 0:
                fwd_copy(2, p, dc // 2, k, dc % 2).start()
            if db == 1 and dc >= 2:
                fin_copy(2, p, 0, k, dc).start()
            if db == 2 and dc < 2:
                fin_copy(2, p, 1, k, dc).start()
    def pass2(j):
        for p in range(3):
            for way in range(2):
                dc = j + 2 * way
                k = slot(p, 3, 1 + way, dc)
                fwd_copy(2, p, way, k, j).wait_recv()
                acc[k, rows_of(p)] = acc[k, rows_of(p)] + fwd2[p][way, j]
                fin_copy(2, p, way, k, dc).start()

    def part3(p, way):
        low, size = ROWS[p]
        return (low, CUT) if way == 0 else (low + CUT, size - CUT)

    def fwd3_copy(p, way):
        low, size = part3(p, way)
        return remote(
            acc.at[slot(p, 3, 3, 0), pl.ds(low, size)], fwd3[p].at[way, pl.ds(0, size)],
            fwd3_send.at[p, way], fwd3_recv.at[p, way], peer((p + 2) % 3, (1, 3)[way]),
        )

    def fin3_copy(p, way, half):
        low, size = part3(p, half)
        return remote(
            acc.at[slot(p, 3, 3, 1 + way), pl.ds(low, size)],
            fin3[p].at[way, pl.ds(low - ROWS[p][0], size)],
            fin3_send.at[p, way, half], fin3_recv.at[p, way, half],
            peer((p + 2) % 3, (1, 3)[way]),
        )

    def gather2(dc):
        for p in range(3):
            k = slot(p, 3, 3, dc)
            for way in range(2):
                fin_copy(2, p, way, k, dc).wait_recv()
            acc[k, rows_of(p)] = acc[k, rows_of(p)] + fin2[p][0, dc] + fin2[p][1, dc]
            if dc == 0:
                fwd3_copy(p, 0).start()
                fwd3_copy(p, 1).start()
            if dc == 1:
                fin3_copy(p, 0, 1).start()
            if dc == 2:
                fin3_copy(p, 1, 0).start()
    def pass3():
        for p in range(3):
            for way in range(2):
                low, size = part3(p, way)
                k = slot(p, 3, 3, 1 + way)
                fwd3_copy(p, way).wait_recv()
                acc[k, pl.ds(low, size)] = acc[k, pl.ds(low, size)] + fwd3[p][way, pl.ds(0, size)]
                fin3_copy(p, way, way).start()

    def gather3():
        for p in range(3):
            for way in range(2):
                for half in range(2):
                    fin3_copy(p, way, half).wait_recv()
            total[rows_of(p)] = acc[63, rows_of(p)] + fin3[p][0] + fin3[p][1]

    d_arrive(4)
    moves = {PACE * (f + 1): functools.partial(gather1, f) for f in range(16)}
    moves |= {SECOND[j]: functools.partial(pass2, j) for j in range(2)}
    moves |= {SECOND[2 + dc]: functools.partial(gather2, dc) for dc in range(4)}
    moves[SECOND[6]] = pass3
    step = 0
    for _ in factorize(diagonal_ref, factor_ref, inverse_ref):
        step += 1
        if step in moves:
            moves.pop(step)()
    for step in sorted(moves):
        moves[step]()
    gather3()
    update_ref[...] = full_dot(inverse_ref[...], total[...])

    for copy in across:
        copy.wait_send()
    for phase in range(5):
        for copy in d_copies(phase):
            copy.wait_send()

    def drain(i, carry):
        for p in range(3):
            for way in range(2):
                fin_copy(1, p, way, 0, i).wait_send()
        return carry

    def drain_half(i, carry):
        for p in range(3):
            for way in range(2):
                fwd_copy(1, p, way, 0, i).wait_send()
        return carry

    lax.fori_loop(0, 16, drain, 0)
    lax.fori_loop(0, 8, drain_half, 0)
    for p in range(3):
        for way in range(2):
            for j in range(2):
                fwd_copy(2, p, way, 0, j).wait_send()
                fin3_copy(p, way, j).wait_send()
            for j in range(4):
                fin_copy(2, p, way, 0, j).wait_send()
            fwd3_copy(p, way).wait_send()


def gather_and_sum(weight, count, lists, strip_columns, tiles):
    blocks, width, rows = strip_columns.shape
    items = tiles.shape[0]
    dma = pltpu.SemaphoreType.DMA
    vmem = lambda *shape: pltpu.VMEM(shape, F32)
    sizes = [size for _, size in ROWS]
    any_space = pl.BlockSpec(memory_space=pl.ANY)
    in_vmem = pl.BlockSpec(memory_space=pltpu.VMEM)
    return pl.pallas_call(
        kernel,
        out_shape=[jax.ShapeDtypeStruct((256, 256), F32)] * 2,
        in_specs=[in_vmem, in_vmem, in_vmem, any_space, any_space],
        out_specs=[in_vmem, in_vmem],
        scratch_shapes=[
            vmem(2 * blocks, width, rows), vmem(2 * blocks, width, rows),
            vmem(2 * items, width, rows),
            pltpu.VMEM((2 * blocks + 2, rows, 4 * width), jnp.bfloat16),
            vmem(2, width, 128), pltpu.VMEM((2, 2, 128), jnp.int32), pltpu.SMEM((2, 2, 128), jnp.int32),
            vmem(64, 256, 256),
            *[vmem(2, 8, s, 256) for s in sizes], *[vmem(2, 16, s, 256) for s in sizes],
            *[vmem(2, 2, s, 256) for s in sizes], *[vmem(2, 4, s, 256) for s in sizes],
            *[vmem(2, CUT, 256) for s in sizes], *[vmem(2, s, 256) for s in sizes],
            vmem(256, 256), vmem(256, 256), vmem(256, 256),
            vmem(256, 256), vmem(7, 32, 256), vmem(32, 256),
            vmem(3, 8, 256), vmem(4, 8, 256), vmem(32, 256),
            dma((4,)), dma((4,)), dma((4,)),
            dma((3, 2, 8)), dma((3, 2, 8)), dma((3, 2, 16)), dma((3, 2, 16)),
            dma((3, 2, 2)), dma((3, 2, 2)), dma((3, 2, 4)), dma((3, 2, 4)),
            dma((3, 2)), dma((3, 2)), dma((3, 2, 2)), dma((3, 2, 2)),
            dma((5, 7)), dma((5, 7)),
        ],
        compiler_params=pltpu.CompilerParams(
            collective_id=0, has_side_effects=True, vmem_limit_bytes=60 << 20
        ),
    )(weight, count, lists, strip_columns, tiles)


def per_device(strip_columns, tile_columns, barrier_weights, column_counts, tile_lists):
    blocks, touched, width, own_width = tile_columns.shape
    return gather_and_sum(
        barrier_weights,
        column_counts.reshape(1, blocks),
        tile_lists,
        strip_columns,
        tile_columns.reshape(blocks * touched, width, own_width),
    )


def solution(mesh):
    return jax.shard_map(
        per_device,
        mesh=mesh,
        in_specs=(
            P(AXES, None, None),
            P(AXES, None, None, None),
            P(AXES, None),
            P(AXES),
            P(AXES, None),
        ),
        out_specs=(P(), P(None, AXES)),
        check_vma=False,
    )
```

```python
import functools

import jax
import jax.numpy as jnp
from jax import lax
from jax.experimental import pallas as pl
from jax.experimental.pallas import tpu as pltpu
from jax.sharding import PartitionSpec as P

AXES = ("row", "col")
MESH = pl.DeviceIdType.MESH
ROWS = ((0, 88), (88, 80), (168, 88))
CUT = 40
PASS = (0, 3, 4, 7, 1, 2, 5, 6)
ORDER = tuple(4 * (j // 2) + j % 2 + 2 * way for j in PASS for way in range(2))
TURNS = (1, 4, 8)
PACE = 5
SECOND = (88, 92, 100, 106, 112, 118, 126)
STRIDE = (16, 4, 1)
F32 = jnp.float32


def split(x):
    high = x.astype(jnp.bfloat16)
    return high, (x - high.astype(F32)).astype(jnp.bfloat16)


def dot(a, b):
    return lax.dot_general(a, b, (((1,), (0,)), ((), ())), preferred_element_type=F32)


def full_dot(a, b, turned=False):
    return lax.dot_general(
        a, b, (((1,), (1 if turned else 0,)), ((), ())),
        precision=lax.Precision.HIGHEST, preferred_element_type=F32,
    )


def diagonal_of(r):
    i = lax.broadcasted_iota(jnp.int32, (r, r), 0)
    return i, lax.broadcasted_iota(jnp.int32, (r, r), 1)


def open_block(a):
    i, j = diagonal_of(128)
    both = jnp.concatenate([a, jnp.where(i == j, 1.0, 0.0)], axis=1)
    return [both[8 * g : 8 * g + 8] for g in range(16)]


def eliminate(groups):
    below = lax.broadcasted_iota(jnp.int32, (8, 1), 0)
    for k in range(0, 128, 2):
        top, s = k // 8, k % 8
        one, two = groups[top][s : s + 1], groups[top][s + 1 : s + 2]
        a, b, c = one[:, k : k + 1], one[:, k + 1 : k + 2], two[:, k + 1 : k + 2]
        first = 1.0 / a
        second = a / (a * c - b * b)
        ratio = b * first
        scaled_one, scaled_two = one * first, (two - ratio * one) * second
        for g in range(top, 16):
            left = groups[g][:, k : k + 1]
            right = groups[g][:, k + 1 : k + 2] - ratio * left
            if g == top:
                left = jnp.where(below > s, left, 0.0)
                right = jnp.where(below > s + 1, right, 0.0)
            groups[g] = groups[g] - left * scaled_one - right * scaled_two
        yield


def close_block(groups):
    both = jnp.concatenate(groups, axis=0)
    i, j = diagonal_of(128)
    pivots = jnp.sum(jnp.where(i == j, both[:, :128], 0.0), axis=1, keepdims=True)
    both = both * (1.0 / jnp.sqrt(pivots))
    return jnp.where(j >= i, both[:, :128], 0.0).T, both[:, 128:]


def factorize(d_ref, l_ref, inverse_ref):
    groups = open_block(d_ref[:128, :128])
    yield from eliminate(groups)
    upper, upper_inverse = close_block(groups)
    between = full_dot(d_ref[128:, :128], upper_inverse, True)
    zero = jnp.zeros((128, 128), F32)
    l_ref[:128, :128] = upper
    l_ref[:128, 128:] = zero
    l_ref[128:, :128] = between
    inverse_ref[:128, :128] = upper_inverse
    inverse_ref[:128, 128:] = zero
    groups = open_block(d_ref[128:, 128:] - full_dot(between, between, True))
    yield from eliminate(groups)
    lower, lower_inverse = close_block(groups)
    l_ref[128:, 128:] = lower
    inverse_ref[128:, 128:] = lower_inverse
    inverse_ref[128:, :128] = -full_dot(
        lower_inverse, full_dot(l_ref[128:, :128], inverse_ref[:128, :128])
    )


def kernel(
    weight_ref, count_ref, list_ref, strip_ref, tile_ref, factor_ref, inverse_ref, sum_ref,
    strip, scaled, tile, left, lives, slots, table, acc,
    fwd1, fin1, fwd2, fin2, fwd3, fin3,
    diagonal_ref, dfull, dx, dquarter, dy, dz, dquarter2,
    load_sem, sib_send, sib_recv,
    fwd1_recv, fin1_recv, fwd2_recv, fin2_recv, out_send, last_recv,
    d_send, d_recv,
):
    row, col = lax.axis_index("row"), lax.axis_index("col")
    core = lax.rem(row, 2)
    place = (lax.div(row, 2), lax.div(col, 4), lax.rem(col, 4))
    blocks, items, width = strip_ref.shape[0], tile_ref.shape[0], strip_ref.shape[1]

    def device(y, x, z, c):
        return (y * 2 + c, x * 4 + z)

    def peer(axis, step):
        at = list(place)
        at[axis] = lax.rem(at[axis] + step, 4)
        return device(*at, core)

    sibling = device(*place, 1 - core)

    def plane_peer(step, flip):
        return device(
            place[0], lax.rem(place[1] + step, 4), place[2], 1 - core if flip else core
        )

    around = [(step, flip) for step in range(4) for flip in (0, 1) if step or flip]

    barrier = pltpu.get_barrier_semaphore()
    partners = [peer(a, s) for a in (0, 2) for s in (1, 2, 3)] + [plane_peer(*at) for at in around]
    for partner in partners:
        pl.semaphore_signal(barrier, inc=1, device_id=partner, device_id_type=MESH)
    get_strip = pltpu.make_async_copy(strip_ref, strip.at[pl.ds(0, blocks)], load_sem.at[0])
    get_tile = pltpu.make_async_copy(tile_ref, tile.at[pl.ds(0, items)], load_sem.at[1])
    get_strip.start()
    get_tile.start()

    lane = lax.broadcasted_iota(jnp.int32, (blocks, 128), 1)
    block = lax.broadcasted_iota(jnp.int32, (blocks, 128), 0)
    least = jnp.full((blocks, 128), items, jnp.int32)
    most = jnp.full((blocks, 128), -1, jnp.int32)
    lists = list_ref[...].T
    for k in range(4):
        listed = lists[:, k : k + 1] == lane
        number = block * 4 + k
        least = jnp.minimum(least, jnp.where(listed, number, items))
        most = jnp.maximum(most, jnp.where(listed, number, -1))
    least = jnp.min(least, axis=0, keepdims=True)
    most = jnp.max(most, axis=0, keepdims=True)
    slots[0, 0:1] = least
    slots[0, 1:2] = jnp.where((most == least) | (most < 0), items, most)
    own_table = pltpu.make_async_copy(slots.at[0], table.at[0], load_sem.at[2])
    own_table.start()

    column = lax.broadcasted_iota(jnp.int32, (width, blocks), 0)
    lives[0] = jnp.zeros(lives.shape[1:], F32)
    lives[0, :, :blocks] = jnp.where(column < count_ref[...], weight_ref[...].T, 0.0)
    pl.semaphore_wait(barrier, len(partners))

    def remote(src, dst, send, recv, to):
        return pltpu.make_async_remote_copy(
            src_ref=src, dst_ref=dst, send_sem=send, recv_sem=recv,
            device_id=to, device_id_type=MESH,
        )

    def build(first, skip):
        def body(q, carry):
            for n in range(4):
                b = first + 4 * q + n
                high = scaled[b].astype(jnp.bfloat16).astype(F32)
                low = scaled[b] - high
                stack = jnp.concatenate([high, high, low, low], axis=0)
                left[b + skip] = stack.T.astype(jnp.bfloat16)
            return carry

        lax.fori_loop(0, blocks // 4, body, 0)

    def weigh(n):
        live = lives[n]
        for b in range(blocks):
            scaled[n * blocks + b] = strip[n * blocks + b] * live[:, b : b + 1]

    across = [
        remote(src, dst, sib_send.at[n], sib_recv.at[n], sibling)
        for n, (src, dst) in enumerate([
            (lives.at[0], lives.at[1]),
            (strip_ref, strip.at[pl.ds(blocks, blocks)]),
            (slots.at[0], slots.at[1]),
            (tile_ref, tile.at[pl.ds(items, items)]),
        ])
    ]
    for copy in across:
        copy.start()
    zero = jnp.zeros(left.shape[1:], left.dtype)
    left[blocks] = zero
    left[2 * blocks + 1] = zero
    get_strip.wait()
    weigh(0)
    build(0, 0)

    def product(ty, tx, tz):
        number = ((ty * 2 + core) * 4 + tx) * 4 + tz
        lefts, rights = [], []
        for n in range(4):
            slot = table[n // 2, n % 2, number]
            lefts.append(left[lax.div(slot, 4) + (n // 2) * (blocks + 1)])
            high, low = split(tile[lax.rem(slot, items) + (n // 2) * items])
            rights += [high, low, high, low]
        return dot(jnp.concatenate(lefts, axis=1), jnp.concatenate(rights, axis=0))

    def offset(d):
        return jnp.where(d == 0, 2, jnp.where(d == 1, 1, jnp.where(d == 2, 3, 0)))

    def group_digits(i):
        turn, at = lax.div(i, 4), lax.rem(i, 4)
        y = jnp.where(at == 0, 0, jnp.where(at == 1, 3, at - 1))
        return [(y, x, lax.rem(turn + 8 - y - x, 4)) for x in range(4)]

    def rows_of(p):
        return pl.ds(*ROWS[p])

    def fwd_copy(stage, p, way, k, j):
        fwd, recv = ((fwd1, fwd1_recv), (fwd2, fwd2_recv))[stage - 1]
        return remote(
            acc.at[k, rows_of(p)], fwd.at[way, j, rows_of(p)],
            out_send.at[2 * stage - 2], recv.at[j], peer((p + stage - 1) % 3, 1 + 2 * way),
        )

    def fin_copy(stage, p, way, k, j):
        fin, recv = ((fin1, fin1_recv), (fin2, fin2_recv))[stage - 1]
        return remote(
            acc.at[k, rows_of(p)], fin.at[way, j, rows_of(p)],
            out_send.at[2 * stage - 1], recv.at[j], peer((p + stage - 1) % 3, 1 + 2 * way),
        )

    def all_here(buffer, recv):
        remote(buffer, buffer, out_send.at[0], recv, sibling).wait_recv()

    def all_gone(buffer, send):
        remote(buffer, buffer, send, last_recv.at[0], sibling).wait_send()

    def send_on(k, digit):
        for p in range(3):
            da, db, dc = digit[p], digit[(p + 1) % 3], digit[(p + 2) % 3]

            if isinstance(da, int):
                da = jnp.int32(da)

            @pl.when(da == 0)
            def _():
                way = jnp.where(dc < 2, 0, 1)
                fwd_copy(1, p, way, k, db * 2 + lax.rem(dc, 2)).start()

            @pl.when(((da == 1) & (dc >= 2)) | ((da == 2) & (dc < 2)))
            def _():
                fin_copy(1, p, da - 1, k, db * 4 + dc).start()

    def tiles(i, carry):
        group = group_digits(i)
        at = [y * 16 + x * 4 + z for y, x, z in group]
        for k, digit in zip(at, group):
            acc[k] = product(*[lax.rem(place[a] + offset(digit[a]), 4) for a in range(3)])
        for k, digit in zip(at, group):
            send_on(k, digit)
        for phase, after in enumerate(TURNS):
            @pl.when(i == after)
            def _():
                d_arrive(phase + 1)
                d_start(phase + 2)

        return carry

    def diagonal_local(b, carry):
        lefts, rights = [], []
        for n in range(2):
            lefts.append(left[2 * b + n])
            high, low = split(strip[2 * b + n])
            rights += [high, low, high, low]
        dfull[...] = dfull[...] + dot(
            jnp.concatenate(lefts, axis=1), jnp.concatenate(rights, axis=0)
        )
        return carry

    py, px, pz = place
    mine = pl.ds(pl.multiple_of(64 * px + 32 * core, 32), 32)

    def d_copies(phase):
        out = []
        if phase in (0, 4):
            for n, (step, flip) in enumerate(around):
                there = 2 * lax.rem(px + step, 4) + (1 - core if flip else core)
                if phase == 0:
                    src, dst = dfull.at[pl.ds(pl.multiple_of(32 * there, 32), 32)], dx.at[n]
                else:
                    src = dst = diagonal_ref.at[mine]
                out.append(remote(src, dst, d_send.at[phase], d_recv.at[phase], plane_peer(step, flip)))
            return out
        for o in (1, 2, 3):
            if phase == 1:
                src, dst, axis = dquarter.at[pl.ds(8 * lax.rem(py + o, 4), 8)], dy.at[o - 1], 0
            elif phase == 2:
                src, dst, axis = dz.at[pz], dz.at[pz], 2
            else:
                part = pl.ds(8 * py, 8)
                src, dst, axis = dquarter2.at[part], dquarter2.at[part], 0
            out.append(remote(src, dst, d_send.at[phase], d_recv.at[phase], peer(axis, o)))
        return out

    def d_bytes(phase):
        return (dx, dy, dz.at[pl.ds(0, 3)], dquarter2.at[pl.ds(0, 24)], diagonal_ref.at[pl.ds(0, 224)])[phase]

    def d_arrive(phase):
        all_here(d_bytes(phase), d_recv.at[phase])
        if phase == 0:
            held = dfull[mine]
            for n in range(len(around)):
                held = held + dx[n]
            dquarter[...] = held
        elif phase == 1:
            dz[pz] = dquarter[pl.ds(8 * py, 8)] + dy[0] + dy[1] + dy[2]
        elif phase == 2:
            dquarter2[pl.ds(8 * py, 8)] = dz[0] + dz[1] + dz[2] + dz[3]
        elif phase == 3:
            diagonal_ref[mine] = dquarter2[...]

    def d_start(phase):
        for copy in d_copies(phase):
            copy.start()

    dfull[...] = jnp.zeros_like(dfull)
    lax.fori_loop(0, blocks // 2, diagonal_local, 0)
    d_start(0)
    across[0].wait_recv()
    across[1].wait_recv()
    weigh(1)
    build(blocks, 1)
    across[2].wait_recv()
    their_table = pltpu.make_async_copy(slots.at[1], table.at[1], load_sem.at[3])
    their_table.start()
    d_arrive(0)
    d_start(1)
    own_table.wait()
    their_table.wait()
    get_tile.wait()
    across[3].wait_recv()
    lax.fori_loop(0, 16, tiles, 0)

    def slot(p, da, db, dc):
        digit = [0, 0, 0]
        digit[p], digit[(p + 1) % 3], digit[(p + 2) % 3] = da, db, dc
        return digit[0] * 16 + digit[1] * 4 + digit[2]

    for j in PASS:
        db = j // 2
        all_here(fwd1.at[:, j], fwd1_recv.at[j])
        for p in range(3):
            for way in range(2):
                dc = j % 2 + 2 * way
                k = slot(p, 1 + way, db, dc)
                acc[k, rows_of(p)] = acc[k, rows_of(p)] + fwd1[way, j, rows_of(p)]
                fin_copy(1, p, way, k, db * 4 + dc).start()

    def gather1(f):
        db, dc = f // 4, f % 4
        all_here(fin1.at[:, f], fin1_recv.at[f])
        for p in range(3):
            k = slot(p, 3, db, dc)
            acc[k, rows_of(p)] = acc[k, rows_of(p)] + fin1[0, f, rows_of(p)] + fin1[1, f, rows_of(p)]
            if db == 0:
                fwd_copy(2, p, dc // 2, k, dc % 2).start()
            if db == 1 and dc >= 2:
                fin_copy(2, p, 0, k, dc).start()
            if db == 2 and dc < 2:
                fin_copy(2, p, 1, k, dc).start()

    def pass2(j):
        all_here(fwd2.at[:, j], fwd2_recv.at[j])
        for p in range(3):
            for way in range(2):
                dc = j + 2 * way
                k = slot(p, 3, 1 + way, dc)
                acc[k, rows_of(p)] = acc[k, rows_of(p)] + fwd2[way, j, rows_of(p)]
                fin_copy(2, p, way, k, dc).start()

    def part3(p, way):
        low, size = ROWS[p]
        return (low, CUT) if way == 0 else (low + CUT, size - CUT)

    def fwd3_copy(p, way):
        rows = pl.ds(*part3(p, way))
        return remote(
            acc.at[slot(p, 3, 3, 0), rows], fwd3.at[rows],
            out_send.at[4], last_recv.at[0], peer((p + 2) % 3, 1 + 2 * way),
        )

    def fin3_copy(p, way, half):
        rows = pl.ds(*part3(p, half))
        return remote(
            acc.at[slot(p, 3, 3, 1 + way), rows], fin3.at[way, rows],
            out_send.at[5], last_recv.at[1], peer((p + 2) % 3, 1 + 2 * way),
        )

    def gather2(dc):
        all_here(fin2.at[:, dc], fin2_recv.at[dc])
        for p in range(3):
            k = slot(p, 3, 3, dc)
            acc[k, rows_of(p)] = acc[k, rows_of(p)] + fin2[0, dc, rows_of(p)] + fin2[1, dc, rows_of(p)]
            if dc == 0:
                fwd3_copy(p, 0).start()
                fwd3_copy(p, 1).start()
            if dc == 1:
                fin3_copy(p, 0, 1).start()
            if dc == 2:
                fin3_copy(p, 1, 0).start()

    def pass3():
        all_here(fwd3, last_recv.at[0])
        for p in range(3):
            for way in range(2):
                rows = pl.ds(*part3(p, way))
                k = slot(p, 3, 3, 1 + way)
                acc[k, rows] = acc[k, rows] + fwd3[rows]
                fin3_copy(p, way, way).start()

    def gather3():
        all_here(fin3, last_recv.at[1])
        sum_ref[...] = acc[63] + fin3[0] + fin3[1]

    d_arrive(4)
    moves = {PACE * (n + 1): functools.partial(gather1, f) for n, f in enumerate(ORDER)}
    moves |= {SECOND[j]: functools.partial(pass2, j) for j in range(2)}
    moves |= {SECOND[2 + dc]: functools.partial(gather2, dc) for dc in range(4)}
    moves[SECOND[6]] = pass3
    step = 0
    for _ in factorize(diagonal_ref, factor_ref, inverse_ref):
        step += 1
        if step in moves:
            moves.pop(step)()
    for step in sorted(moves):
        moves[step]()
    gather3()

    for copy in across:
        copy.wait_send()
    for phase in range(5):
        all_gone(d_bytes(phase), d_send.at[phase])
    for n, buffer in enumerate((fwd1, fin1, fwd2, fin2, fwd3, fin3)):
        all_gone(buffer, out_send.at[n])


def finish(factor_ref, inverse_ref, sum_ref, factor_out, update_out):
    factor_out[...] = factor_ref[...]
    update_out[...] = full_dot(inverse_ref[...], sum_ref[...])


def gather_and_sum(weight, count, lists, strip_columns, tiles):
    blocks, width, rows = strip_columns.shape
    items = tiles.shape[0]
    dma = pltpu.SemaphoreType.DMA
    vmem = lambda *shape: pltpu.VMEM(shape, F32)
    any_space = pl.BlockSpec(memory_space=pl.ANY)
    in_vmem = pl.BlockSpec(memory_space=pltpu.VMEM)
    return pl.pallas_call(
        kernel,
        out_shape=[jax.ShapeDtypeStruct((256, 256), F32)] * 3,
        in_specs=[in_vmem, in_vmem, in_vmem, any_space, any_space],
        out_specs=[in_vmem] * 3,
        scratch_shapes=[
            vmem(2 * blocks, width, rows), vmem(2 * blocks, width, rows),
            vmem(2 * items, width, rows),
            pltpu.VMEM((2 * blocks + 2, rows, 4 * width), jnp.bfloat16),
            vmem(2, width, 128), pltpu.VMEM((2, 2, 128), jnp.int32), pltpu.SMEM((2, 2, 128), jnp.int32),
            vmem(64, 256, 256),
            vmem(2, 8, 256, 256), vmem(2, 16, 256, 256), vmem(2, 2, 256, 256), vmem(2, 4, 256, 256),
            vmem(256, 256), vmem(2, 256, 256),
            vmem(256, 256),
            vmem(256, 256), vmem(7, 32, 256), vmem(32, 256),
            vmem(3, 8, 256), vmem(4, 8, 256), vmem(32, 256),
            dma((4,)), dma((4,)), dma((4,)),
            dma((8,)), dma((16,)), dma((2,)), dma((4,)), dma((6,)), dma((2,)),
            dma((5,)), dma((5,)),
        ],
        compiler_params=pltpu.CompilerParams(
            collective_id=0, has_side_effects=True, vmem_limit_bytes=60 << 20
        ),
    )(weight, count, lists, strip_columns, tiles)


def per_device(strip_columns, tile_columns, barrier_weights, column_counts, tile_lists):
    blocks, touched, width, own_width = tile_columns.shape
    in_vmem = pl.BlockSpec(memory_space=pltpu.VMEM)
    parts = gather_and_sum(
        barrier_weights,
        column_counts.reshape(1, blocks),
        tile_lists.T,
        strip_columns,
        tile_columns.reshape(blocks * touched, width, own_width),
    )
    return pl.pallas_call(
        finish,
        out_shape=[jax.ShapeDtypeStruct((256, 256), F32)] * 2,
        in_specs=[in_vmem] * 3,
        out_specs=[in_vmem] * 2,
    )(*parts)


def solution(mesh):
    return jax.shard_map(
        per_device,
        mesh=mesh,
        in_specs=(
            P(AXES, None, None),
            P(AXES, None, None, None),
            P(AXES, None),
            P(AXES),
            P(AXES, None),
        ),
        out_specs=(P(), P(None, AXES)),
        check_vma=False,
    )
```

```python
import functools

import jax
import jax.numpy as jnp
from jax import lax
from jax.experimental import pallas as pl
from jax.experimental.pallas import tpu as pltpu
from jax.sharding import PartitionSpec as P

AXES = ("row", "col")
MESH = pl.DeviceIdType.MESH
ROWS = ((0, 88), (88, 80), (168, 88))
CUT = 40
PASS = (0, 3, 4, 7, 1, 2, 5, 6)
ORDER = tuple(4 * (j // 2) + j % 2 + 2 * way for j in PASS for way in range(2))
TURNS = (1, 4, 8)
EARLY = 4
WHEN = (24, 30, 36, 42, 50, 55, 60, 65, 70, 75, 80, 85, 90, 95, 100, 105, 110, 115, 120, 125)
STRIDE = (16, 4, 1)
F32 = jnp.float32


def split(x):
    high = x.astype(jnp.bfloat16)
    return high, (x - high.astype(F32)).astype(jnp.bfloat16)


def dot(a, b):
    return lax.dot_general(a, b, (((1,), (0,)), ((), ())), preferred_element_type=F32)


def full_dot(a, b, turned=False):
    return lax.dot_general(
        a, b, (((1,), (1 if turned else 0,)), ((), ())),
        precision=lax.Precision.HIGHEST, preferred_element_type=F32,
    )


def diagonal_of(r):
    i = lax.broadcasted_iota(jnp.int32, (r, r), 0)
    return i, lax.broadcasted_iota(jnp.int32, (r, r), 1)


def open_block(a):
    i, j = diagonal_of(128)
    both = jnp.concatenate([a, jnp.where(i == j, 1.0, 0.0)], axis=1)
    return [both[8 * g : 8 * g + 8] for g in range(16)]


def eliminate(groups):
    below = lax.broadcasted_iota(jnp.int32, (8, 1), 0)
    for k in range(0, 128, 2):
        top, s = k // 8, k % 8
        one, two = groups[top][s : s + 1], groups[top][s + 1 : s + 2]
        a, b, c = one[:, k : k + 1], one[:, k + 1 : k + 2], two[:, k + 1 : k + 2]
        first = 1.0 / a
        second = a / (a * c - b * b)
        ratio = b * first
        scaled_one, scaled_two = one * first, (two - ratio * one) * second
        for g in range(top, 16):
            left = groups[g][:, k : k + 1]
            right = groups[g][:, k + 1 : k + 2] - ratio * left
            if g == top:
                left = jnp.where(below > s, left, 0.0)
                right = jnp.where(below > s + 1, right, 0.0)
            groups[g] = groups[g] - left * scaled_one - right * scaled_two
        yield


def close_block(groups):
    both = jnp.concatenate(groups, axis=0)
    i, j = diagonal_of(128)
    pivots = jnp.sum(jnp.where(i == j, both[:, :128], 0.0), axis=1, keepdims=True)
    both = both * (1.0 / jnp.sqrt(pivots))
    return jnp.where(j >= i, both[:, :128], 0.0).T, both[:, 128:]


def factorize(d_ref, l_ref, inverse_ref):
    groups = open_block(d_ref[:128, :128])
    yield from eliminate(groups)
    upper, upper_inverse = close_block(groups)
    between = full_dot(d_ref[128:, :128], upper_inverse, True)
    zero = jnp.zeros((128, 128), F32)
    l_ref[:128, :128] = upper
    l_ref[:128, 128:] = zero
    l_ref[128:, :128] = between
    inverse_ref[:128, :128] = upper_inverse
    inverse_ref[:128, 128:] = zero
    groups = open_block(d_ref[128:, 128:] - full_dot(between, between, True))
    yield from eliminate(groups)
    lower, lower_inverse = close_block(groups)
    l_ref[128:, 128:] = lower
    inverse_ref[128:, 128:] = lower_inverse
    inverse_ref[128:, :128] = -full_dot(
        lower_inverse, full_dot(l_ref[128:, :128], inverse_ref[:128, :128])
    )


def kernel(
    weight_ref, count_ref, list_ref, strip_ref, tile_ref, factor_ref, inverse_ref, sum_ref,
    strip, scaled, tile, left, lives, slots, table, acc,
    fwd1, fin1, fwd2, fin2, fwd3, fin3,
    diagonal_ref, dfull, dx, dquarter, dy, dz, dquarter2,
    load_sem, sib_send, sib_recv,
    fwd1_recv, fin1_recv, fwd2_recv, fin2_recv, out_send, last_recv,
    d_send, d_recv,
):
    row, col = lax.axis_index("row"), lax.axis_index("col")
    core = lax.rem(row, 2)
    place = (lax.div(row, 2), lax.div(col, 4), lax.rem(col, 4))
    blocks, items, width = strip_ref.shape[0], tile_ref.shape[0], strip_ref.shape[1]

    def device(y, x, z, c):
        return (y * 2 + c, x * 4 + z)

    def peer(axis, step):
        at = list(place)
        at[axis] = lax.rem(at[axis] + step, 4)
        return device(*at, core)

    sibling = device(*place, 1 - core)

    def plane_peer(step, flip):
        return device(
            place[0], lax.rem(place[1] + step, 4), place[2], 1 - core if flip else core
        )

    around = [(step, flip) for step in range(4) for flip in (0, 1) if step or flip]

    barrier = pltpu.get_barrier_semaphore()
    partners = [peer(a, s) for a in (0, 2) for s in (1, 2, 3)] + [plane_peer(*at) for at in around]
    for partner in partners:
        pl.semaphore_signal(barrier, inc=1, device_id=partner, device_id_type=MESH)
    get_strip = pltpu.make_async_copy(strip_ref, strip.at[pl.ds(0, blocks)], load_sem.at[0])
    get_tile = pltpu.make_async_copy(tile_ref, tile.at[pl.ds(0, items)], load_sem.at[1])
    get_strip.start()
    get_tile.start()

    lane = lax.broadcasted_iota(jnp.int32, (blocks, 128), 1)
    block = lax.broadcasted_iota(jnp.int32, (blocks, 128), 0)
    least = jnp.full((blocks, 128), items, jnp.int32)
    most = jnp.full((blocks, 128), -1, jnp.int32)
    lists = list_ref[...].T
    for k in range(4):
        listed = lists[:, k : k + 1] == lane
        number = block * 4 + k
        least = jnp.minimum(least, jnp.where(listed, number, items))
        most = jnp.maximum(most, jnp.where(listed, number, -1))
    least = jnp.min(least, axis=0, keepdims=True)
    most = jnp.max(most, axis=0, keepdims=True)
    slots[0, 0:1] = least
    slots[0, 1:2] = jnp.where((most == least) | (most < 0), items, most)
    own_table = pltpu.make_async_copy(slots.at[0], table.at[0], load_sem.at[2])
    own_table.start()

    column = lax.broadcasted_iota(jnp.int32, (width, blocks), 0)
    lives[0] = jnp.zeros(lives.shape[1:], F32)
    lives[0, :, :blocks] = jnp.where(column < count_ref[...], weight_ref[...].T, 0.0)
    pl.semaphore_wait(barrier, len(partners))

    def remote(src, dst, send, recv, to):
        return pltpu.make_async_remote_copy(
            src_ref=src, dst_ref=dst, send_sem=send, recv_sem=recv,
            device_id=to, device_id_type=MESH,
        )

    def build(first, skip):
        def body(q, carry):
            for n in range(4):
                b = first + 4 * q + n
                high = scaled[b].astype(jnp.bfloat16).astype(F32)
                low = scaled[b] - high
                stack = jnp.concatenate([high, high, low, low], axis=0)
                left[b + skip] = stack.T.astype(jnp.bfloat16)
            return carry

        lax.fori_loop(0, blocks // 4, body, 0)

    def weigh(n):
        live = lives[n]
        for b in range(blocks):
            scaled[n * blocks + b] = strip[n * blocks + b] * live[:, b : b + 1]

    across = [
        remote(src, dst, sib_send.at[n], sib_recv.at[n], sibling)
        for n, (src, dst) in enumerate([
            (lives.at[0], lives.at[1]),
            (strip_ref, strip.at[pl.ds(blocks, blocks)]),
            (slots.at[0], slots.at[1]),
            (tile_ref, tile.at[pl.ds(items, items)]),
        ])
    ]
    for copy in across:
        copy.start()
    zero = jnp.zeros(left.shape[1:], left.dtype)
    left[blocks] = zero
    left[2 * blocks + 1] = zero
    get_strip.wait()
    weigh(0)
    build(0, 0)

    def product(ty, tx, tz):
        number = ((ty * 2 + core) * 4 + tx) * 4 + tz
        lefts, rights = [], []
        for n in range(4):
            slot = table[n // 2, n % 2, number]
            lefts.append(left[lax.div(slot, 4) + (n // 2) * (blocks + 1)])
            high, low = split(tile[lax.rem(slot, items) + (n // 2) * items])
            rights += [high, low, high, low]
        return dot(jnp.concatenate(lefts, axis=1), jnp.concatenate(rights, axis=0))

    def offset(d):
        return jnp.where(d == 0, 2, jnp.where(d == 1, 1, jnp.where(d == 2, 3, 0)))

    def group_digits(i):
        turn, at = lax.div(i, 4), lax.rem(i, 4)
        y = jnp.where(at == 1, 2, jnp.where(at == 2, 1, at))
        return [(y, x, lax.rem(turn + 8 - y - x, 4)) for x in range(4)]

    def rows_of(p):
        return pl.ds(*ROWS[p])

    def fwd_copy(stage, p, way, k, j):
        fwd, recv = ((fwd1, fwd1_recv), (fwd2, fwd2_recv))[stage - 1]
        return remote(
            acc.at[k, rows_of(p)], fwd.at[way, j, rows_of(p)],
            out_send.at[2 * stage - 2], recv.at[j], peer((p + stage - 1) % 3, 1 + 2 * way),
        )

    def fin_copy(stage, p, way, k, j):
        fin, recv = ((fin1, fin1_recv), (fin2, fin2_recv))[stage - 1]
        return remote(
            acc.at[k, rows_of(p)], fin.at[way, j, rows_of(p)],
            out_send.at[2 * stage - 1], recv.at[j], peer((p + stage - 1) % 3, 1 + 2 * way),
        )

    def all_here(buffer, recv):
        remote(buffer, buffer, out_send.at[0], recv, sibling).wait_recv()

    def all_gone(buffer, send):
        remote(buffer, buffer, send, last_recv.at[0], sibling).wait_send()

    def send_on(k, digit):
        for p in range(3):
            da, db, dc = digit[p], digit[(p + 1) % 3], digit[(p + 2) % 3]

            if isinstance(da, int):
                da = jnp.int32(da)

            @pl.when(da == 0)
            def _():
                way = jnp.where(dc < 2, 0, 1)
                fwd_copy(1, p, way, k, db * 2 + lax.rem(dc, 2)).start()

            @pl.when(((da == 1) & (dc >= 2)) | ((da == 2) & (dc < 2)))
            def _():
                fin_copy(1, p, da - 1, k, db * 4 + dc).start()

    def tiles(i, carry):
        group = group_digits(i)
        at = [y * 16 + x * 4 + z for y, x, z in group]
        for k, digit in zip(at, group):
            acc[k] = product(*[lax.rem(place[a] + offset(digit[a]), 4) for a in range(3)])
        for k, digit in zip(at, group):
            send_on(k, digit)
        for phase, after in enumerate(TURNS):
            @pl.when(i == after)
            def _():
                d_arrive(phase + 1)
                d_start(phase + 2)

        return carry

    def diagonal_local(b, carry):
        lefts, rights = [], []
        for n in range(2):
            lefts.append(left[2 * b + n])
            high, low = split(strip[2 * b + n])
            rights += [high, low, high, low]
        dfull[...] = dfull[...] + dot(
            jnp.concatenate(lefts, axis=1), jnp.concatenate(rights, axis=0)
        )
        return carry

    py, px, pz = place
    mine = pl.ds(pl.multiple_of(64 * px + 32 * core, 32), 32)

    def d_copies(phase):
        out = []
        if phase in (0, 4):
            for n, (step, flip) in enumerate(around):
                there = 2 * lax.rem(px + step, 4) + (1 - core if flip else core)
                if phase == 0:
                    src, dst = dfull.at[pl.ds(pl.multiple_of(32 * there, 32), 32)], dx.at[n]
                else:
                    src = dst = diagonal_ref.at[mine]
                out.append(remote(src, dst, d_send.at[phase], d_recv.at[phase], plane_peer(step, flip)))
            return out
        for o in (1, 2, 3):
            if phase == 1:
                src, dst, axis = dquarter.at[pl.ds(8 * lax.rem(py + o, 4), 8)], dy.at[o - 1], 0
            elif phase == 2:
                src, dst, axis = dz.at[pz], dz.at[pz], 2
            else:
                part = pl.ds(8 * py, 8)
                src, dst, axis = dquarter2.at[part], dquarter2.at[part], 0
            out.append(remote(src, dst, d_send.at[phase], d_recv.at[phase], peer(axis, o)))
        return out

    def d_bytes(phase):
        return (dx, dy, dz.at[pl.ds(0, 3)], dquarter2.at[pl.ds(0, 24)], diagonal_ref.at[pl.ds(0, 224)])[phase]

    def d_arrive(phase):
        all_here(d_bytes(phase), d_recv.at[phase])
        if phase == 0:
            held = dfull[mine]
            for n in range(len(around)):
                held = held + dx[n]
            dquarter[...] = held
        elif phase == 1:
            dz[pz] = dquarter[pl.ds(8 * py, 8)] + dy[0] + dy[1] + dy[2]
        elif phase == 2:
            dquarter2[pl.ds(8 * py, 8)] = dz[0] + dz[1] + dz[2] + dz[3]
        elif phase == 3:
            diagonal_ref[mine] = dquarter2[...]

    def d_start(phase):
        for copy in d_copies(phase):
            copy.start()

    dfull[...] = jnp.zeros_like(dfull)
    lax.fori_loop(0, blocks // 2, diagonal_local, 0)
    d_start(0)
    across[0].wait_recv()
    across[1].wait_recv()
    weigh(1)
    build(blocks, 1)
    across[2].wait_recv()
    their_table = pltpu.make_async_copy(slots.at[1], table.at[1], load_sem.at[3])
    their_table.start()
    d_arrive(0)
    d_start(1)
    own_table.wait()
    their_table.wait()
    get_tile.wait()
    across[3].wait_recv()
    lax.fori_loop(0, 16, tiles, 0)

    def slot(p, da, db, dc):
        digit = [0, 0, 0]
        digit[p], digit[(p + 1) % 3], digit[(p + 2) % 3] = da, db, dc
        return digit[0] * 16 + digit[1] * 4 + digit[2]

    def pass1(j):
        db = j // 2
        all_here(fwd1.at[:, j], fwd1_recv.at[j])
        for p in range(3):
            for way in range(2):
                dc = j % 2 + 2 * way
                k = slot(p, 1 + way, db, dc)
                acc[k, rows_of(p)] = acc[k, rows_of(p)] + fwd1[way, j, rows_of(p)]
                fin_copy(1, p, way, k, db * 4 + dc).start()

    def gather1(f):
        db, dc = f // 4, f % 4
        all_here(fin1.at[:, f], fin1_recv.at[f])
        for p in range(3):
            k = slot(p, 3, db, dc)
            acc[k, rows_of(p)] = acc[k, rows_of(p)] + fin1[0, f, rows_of(p)] + fin1[1, f, rows_of(p)]
            if db == 0:
                fwd_copy(2, p, dc // 2, k, dc % 2).start()
            if db == 1 and dc >= 2:
                fin_copy(2, p, 0, k, dc).start()
            if db == 2 and dc < 2:
                fin_copy(2, p, 1, k, dc).start()

    def pass2(j):
        all_here(fwd2.at[:, j], fwd2_recv.at[j])
        for p in range(3):
            for way in range(2):
                dc = j + 2 * way
                k = slot(p, 3, 1 + way, dc)
                acc[k, rows_of(p)] = acc[k, rows_of(p)] + fwd2[way, j, rows_of(p)]
                fin_copy(2, p, way, k, dc).start()

    def part3(p, way):
        low, size = ROWS[p]
        return (low, CUT) if way == 0 else (low + CUT, size - CUT)

    def fwd3_copy(p, way):
        rows = pl.ds(*part3(p, way))
        return remote(
            acc.at[slot(p, 3, 3, 0), rows], fwd3.at[rows],
            out_send.at[4], last_recv.at[0], peer((p + 2) % 3, 1 + 2 * way),
        )

    def fin3_copy(p, way, half):
        rows = pl.ds(*part3(p, half))
        return remote(
            acc.at[slot(p, 3, 3, 1 + way), rows], fin3.at[way, rows],
            out_send.at[5], last_recv.at[1], peer((p + 2) % 3, 1 + 2 * way),
        )

    def gather2(dc):
        all_here(fin2.at[:, dc], fin2_recv.at[dc])
        for p in range(3):
            k = slot(p, 3, 3, dc)
            acc[k, rows_of(p)] = acc[k, rows_of(p)] + fin2[0, dc, rows_of(p)] + fin2[1, dc, rows_of(p)]
            if dc == 0:
                fwd3_copy(p, 0).start()
                fwd3_copy(p, 1).start()
            if dc == 1:
                fin3_copy(p, 0, 1).start()
            if dc == 2:
                fin3_copy(p, 1, 0).start()

    def pass3():
        all_here(fwd3, last_recv.at[0])
        for p in range(3):
            for way in range(2):
                rows = pl.ds(*part3(p, way))
                k = slot(p, 3, 3, 1 + way)
                acc[k, rows] = acc[k, rows] + fwd3[rows]
                fin3_copy(p, way, way).start()

    def gather3():
        all_here(fin3, last_recv.at[1])
        sum_ref[...] = acc[63] + fin3[0] + fin3[1]

    events = [functools.partial(pass1, j) for j in PASS]
    events += [functools.partial(gather1, f) for f in ORDER]
    events += [functools.partial(pass2, j) for j in range(2)]
    events += [functools.partial(gather2, dc) for dc in range(4)]
    events += [pass3, gather3]
    for event in events[:EARLY]:
        event()
    d_arrive(4)
    moves = dict(zip(WHEN, events[EARLY:]))
    step = 0
    for _ in factorize(diagonal_ref, factor_ref, inverse_ref):
        step += 1
        if step in moves:
            moves.pop(step)()
    for event in events[EARLY + len(WHEN) - len(moves) :]:
        event()

    for copy in across:
        copy.wait_send()
    for phase in range(5):
        all_gone(d_bytes(phase), d_send.at[phase])
    for n, buffer in enumerate((fwd1, fin1, fwd2, fin2, fwd3, fin3)):
        all_gone(buffer, out_send.at[n])


def finish(factor_ref, inverse_ref, sum_ref, factor_out, update_out):
    factor_out[...] = factor_ref[...]
    update_out[...] = full_dot(inverse_ref[...], sum_ref[...])


def gather_and_sum(weight, count, lists, strip_columns, tiles):
    blocks, width, rows = strip_columns.shape
    items = tiles.shape[0]
    dma = pltpu.SemaphoreType.DMA
    vmem = lambda *shape: pltpu.VMEM(shape, F32)
    any_space = pl.BlockSpec(memory_space=pl.ANY)
    in_vmem = pl.BlockSpec(memory_space=pltpu.VMEM)
    return pl.pallas_call(
        kernel,
        out_shape=[jax.ShapeDtypeStruct((256, 256), F32)] * 3,
        in_specs=[in_vmem, in_vmem, in_vmem, any_space, any_space],
        out_specs=[in_vmem] * 3,
        scratch_shapes=[
            vmem(2 * blocks, width, rows), vmem(2 * blocks, width, rows),
            vmem(2 * items, width, rows),
            pltpu.VMEM((2 * blocks + 2, rows, 4 * width), jnp.bfloat16),
            vmem(2, width, 128), pltpu.VMEM((2, 2, 128), jnp.int32), pltpu.SMEM((2, 2, 128), jnp.int32),
            vmem(64, 256, 256),
            vmem(2, 8, 256, 256), vmem(2, 16, 256, 256), vmem(2, 2, 256, 256), vmem(2, 4, 256, 256),
            vmem(256, 256), vmem(2, 256, 256),
            vmem(256, 256),
            vmem(256, 256), vmem(7, 32, 256), vmem(32, 256),
            vmem(3, 8, 256), vmem(4, 8, 256), vmem(32, 256),
            dma((4,)), dma((4,)), dma((4,)),
            dma((8,)), dma((16,)), dma((2,)), dma((4,)), dma((6,)), dma((2,)),
            dma((5,)), dma((5,)),
        ],
        compiler_params=pltpu.CompilerParams(
            collective_id=0, has_side_effects=True, vmem_limit_bytes=60 << 20
        ),
    )(weight, count, lists, strip_columns, tiles)


def per_device(strip_columns, tile_columns, barrier_weights, column_counts, tile_lists):
    blocks, touched, width, own_width = tile_columns.shape
    in_vmem = pl.BlockSpec(memory_space=pltpu.VMEM)
    parts = gather_and_sum(
        barrier_weights,
        column_counts.reshape(1, blocks),
        tile_lists.T,
        strip_columns,
        tile_columns.reshape(blocks * touched, width, own_width),
    )
    return pl.pallas_call(
        finish,
        out_shape=[jax.ShapeDtypeStruct((256, 256), F32)] * 2,
        in_specs=[in_vmem] * 3,
        out_specs=[in_vmem] * 2,
    )(*parts)


def solution(mesh):
    return jax.shard_map(
        per_device,
        mesh=mesh,
        in_specs=(
            P(AXES, None, None),
            P(AXES, None, None, None),
            P(AXES, None),
            P(AXES),
            P(AXES, None),
        ),
        out_specs=(P(), P(None, AXES)),
        check_vma=False,
    )
```

```python
import functools

import jax
import jax.numpy as jnp
from jax import lax
from jax.experimental import pallas as pl
from jax.experimental.pallas import tpu as pltpu
from jax.sharding import PartitionSpec as P

AXES = ("row", "col")
MESH = pl.DeviceIdType.MESH
ROWS = ((0, 88), (88, 80), (168, 88))
CUT = 40
PASS = (0, 3, 4, 7, 1, 2, 5, 6)
ORDER = tuple(4 * (j // 2) + j % 2 + 2 * way for j in PASS for way in range(2))
TURNS = (3, 9, 15, 21)
EARLY = 4
WHEN = (12, 18, 24, 30, 50, 55, 60, 65, 70, 75, 80, 85, 90, 95, 100, 105, 110, 115, 120, 125)
STRIDE = (16, 4, 1)
F32 = jnp.float32


def split(x):
    high = x.astype(jnp.bfloat16)
    return high, (x - high.astype(F32)).astype(jnp.bfloat16)


def dot(a, b):
    return lax.dot_general(a, b, (((1,), (0,)), ((), ())), preferred_element_type=F32)


def full_dot(a, b, turned=False):
    return lax.dot_general(
        a, b, (((1,), (1 if turned else 0,)), ((), ())),
        precision=lax.Precision.HIGHEST, preferred_element_type=F32,
    )


def diagonal_of(r):
    i = lax.broadcasted_iota(jnp.int32, (r, r), 0)
    return i, lax.broadcasted_iota(jnp.int32, (r, r), 1)


def open_block(a):
    i, j = diagonal_of(128)
    both = jnp.concatenate([a, jnp.where(i == j, 1.0, 0.0)], axis=1)
    return [both[8 * g : 8 * g + 8] for g in range(16)]


def eliminate(groups):
    below = lax.broadcasted_iota(jnp.int32, (8, 1), 0)
    for k in range(0, 128, 2):
        top, s = k // 8, k % 8
        one, two = groups[top][s : s + 1], groups[top][s + 1 : s + 2]
        a, b, c = one[:, k : k + 1], one[:, k + 1 : k + 2], two[:, k + 1 : k + 2]
        first = 1.0 / a
        second = a / (a * c - b * b)
        ratio = b * first
        scaled_one, scaled_two = one * first, (two - ratio * one) * second
        for g in range(top, 16):
            left = groups[g][:, k : k + 1]
            right = groups[g][:, k + 1 : k + 2] - ratio * left
            if g == top:
                left = jnp.where(below > s, left, 0.0)
                right = jnp.where(below > s + 1, right, 0.0)
            groups[g] = groups[g] - left * scaled_one - right * scaled_two
        yield


def close_block(groups):
    both = jnp.concatenate(groups, axis=0)
    i, j = diagonal_of(128)
    pivots = jnp.sum(jnp.where(i == j, both[:, :128], 0.0), axis=1, keepdims=True)
    both = both * (1.0 / jnp.sqrt(pivots))
    return jnp.where(j >= i, both[:, :128], 0.0).T, both[:, 128:]


def factorize(d_ref, l_ref, inverse_ref):
    groups = open_block(d_ref[:128, :128])
    yield from eliminate(groups)
    upper, upper_inverse = close_block(groups)
    between = full_dot(d_ref[128:, :128], upper_inverse, True)
    zero = jnp.zeros((128, 128), F32)
    l_ref[:128, :128] = upper
    l_ref[:128, 128:] = zero
    l_ref[128:, :128] = between
    inverse_ref[:128, :128] = upper_inverse
    inverse_ref[:128, 128:] = zero
    groups = open_block(d_ref[128:, 128:] - full_dot(between, between, True))
    yield from eliminate(groups)
    lower, lower_inverse = close_block(groups)
    l_ref[128:, 128:] = lower
    inverse_ref[128:, 128:] = lower_inverse
    inverse_ref[128:, :128] = -full_dot(
        lower_inverse, full_dot(l_ref[128:, :128], inverse_ref[:128, :128])
    )


def kernel(
    weight_ref, count_ref, list_ref, strip_ref, tile_ref, factor_ref, inverse_ref, sum_ref,
    strip, scaled, tile0, tile1, left, lives, slots, table, acc,
    fwd1, fin1, fwd2, fin2, fwd3, fin3,
    diagonal_ref, dfull, dx, dquarter, dy, dz, dquarter2,
    load_sem, sib_send, sib_recv,
    fwd1_recv, fin1_recv, fwd2_recv, fin2_recv, out_send, last_recv,
    d_send, d_recv,
):
    tile = (tile0, tile1)
    row, col = lax.axis_index("row"), lax.axis_index("col")
    core = lax.rem(row, 2)
    place = (lax.div(row, 2), lax.div(col, 4), lax.rem(col, 4))
    blocks, items, width = strip_ref.shape[0], tile_ref.shape[0], strip_ref.shape[1]

    def device(y, x, z, c):
        return (y * 2 + c, x * 4 + z)

    def peer(axis, step):
        at = list(place)
        at[axis] = lax.rem(at[axis] + step, 4)
        return device(*at, core)

    sibling = device(*place, 1 - core)

    def plane_peer(step, flip):
        return device(
            place[0], lax.rem(place[1] + step, 4), place[2], 1 - core if flip else core
        )

    around = [(step, flip) for step in range(4) for flip in (0, 1) if step or flip]

    barrier = pltpu.get_barrier_semaphore()
    partners = [peer(a, s) for a in (0, 2) for s in (1, 2, 3)] + [plane_peer(*at) for at in around]
    for partner in partners:
        pl.semaphore_signal(barrier, inc=1, device_id=partner, device_id_type=MESH)
    get_strip = pltpu.make_async_copy(strip_ref, strip.at[pl.ds(0, blocks)], load_sem.at[0])
    get_tile = [
        pltpu.make_async_copy(
            tile_ref.at[:, :, pl.ds(128 * h, 128)], tile[h].at[pl.ds(0, items)], load_sem.at[(1, 4)[h]]
        )
        for h in range(2)
    ]
    get_strip.start()
    for copy in get_tile:
        copy.start()

    lane = lax.broadcasted_iota(jnp.int32, (blocks, 128), 1)
    block = lax.broadcasted_iota(jnp.int32, (blocks, 128), 0)
    least = jnp.full((blocks, 128), items, jnp.int32)
    most = jnp.full((blocks, 128), -1, jnp.int32)
    lists = list_ref[...].T
    for k in range(4):
        listed = lists[:, k : k + 1] == lane
        number = block * 4 + k
        least = jnp.minimum(least, jnp.where(listed, number, items))
        most = jnp.maximum(most, jnp.where(listed, number, -1))
    least = jnp.min(least, axis=0, keepdims=True)
    most = jnp.max(most, axis=0, keepdims=True)
    slots[0, 0:1] = least
    slots[0, 1:2] = jnp.where((most == least) | (most < 0), items, most)
    own_table = pltpu.make_async_copy(slots.at[0], table.at[0], load_sem.at[2])
    own_table.start()

    column = lax.broadcasted_iota(jnp.int32, (width, blocks), 0)
    lives[0] = jnp.zeros(lives.shape[1:], F32)
    lives[0, :, :blocks] = jnp.where(column < count_ref[...], weight_ref[...].T, 0.0)
    pl.semaphore_wait(barrier, len(partners))

    def remote(src, dst, send, recv, to):
        return pltpu.make_async_remote_copy(
            src_ref=src, dst_ref=dst, send_sem=send, recv_sem=recv,
            device_id=to, device_id_type=MESH,
        )

    def build(first, skip):
        def body(q, carry):
            for n in range(4):
                b = first + 4 * q + n
                high = scaled[b].astype(jnp.bfloat16).astype(F32)
                low = scaled[b] - high
                stack = jnp.concatenate([high, high, low, low], axis=0)
                left[b + skip] = stack.T.astype(jnp.bfloat16)
            return carry

        lax.fori_loop(0, blocks // 4, body, 0)

    def weigh(n):
        live = lives[n]
        for b in range(blocks):
            scaled[n * blocks + b] = strip[n * blocks + b] * live[:, b : b + 1]

    across = [
        remote(src, dst, sib_send.at[n], sib_recv.at[n], sibling)
        for n, (src, dst) in enumerate([
            (lives.at[0], lives.at[1]),
            (strip_ref, strip.at[pl.ds(blocks, blocks)]),
            (slots.at[0], slots.at[1]),
            *[
                (tile_ref.at[:, :, pl.ds(128 * h, 128)], tile[h].at[pl.ds(items, items)])
                for h in range(2)
            ],
        ])
    ]
    for copy in across:
        copy.start()
    zero = jnp.zeros(left.shape[1:], left.dtype)
    left[blocks] = zero
    left[2 * blocks + 1] = zero
    get_strip.wait()
    weigh(0)
    build(0, 0)

    def product(h, ty, tx, tz):
        number = ((ty * 2 + core) * 4 + tx) * 4 + tz
        lefts, rights = [], []
        for n in range(4):
            slot = table[n // 2, n % 2, number]
            lefts.append(left[lax.div(slot, 4) + (n // 2) * (blocks + 1)])
            high, low = split(tile[h][lax.rem(slot, items) + (n // 2) * items])
            rights += [high, low, high, low]
        return dot(jnp.concatenate(lefts, axis=1), jnp.concatenate(rights, axis=0))

    def offset(d):
        return jnp.where(d == 0, 2, jnp.where(d == 1, 1, jnp.where(d == 2, 3, 0)))

    def group_digits(i):
        turn, at = lax.div(i, 4), lax.rem(i, 4)
        y = jnp.where(at == 1, 2, jnp.where(at == 2, 1, at))
        return [(y, x, lax.rem(turn + 8 - y - x, 4)) for x in range(4)]

    def rows_of(p):
        return pl.ds(*ROWS[p])

    def fwd_copy(stage, p, way, k, j, columns=pl.ds(0, 256)):
        fwd, recv = ((fwd1, fwd1_recv), (fwd2, fwd2_recv))[stage - 1]
        return remote(
            acc.at[k, rows_of(p), columns], fwd.at[way, j, rows_of(p), columns],
            out_send.at[2 * stage - 2], recv.at[j], peer((p + stage - 1) % 3, 1 + 2 * way),
        )

    def fin_copy(stage, p, way, k, j, columns=pl.ds(0, 256)):
        fin, recv = ((fin1, fin1_recv), (fin2, fin2_recv))[stage - 1]
        return remote(
            acc.at[k, rows_of(p), columns], fin.at[way, j, rows_of(p), columns],
            out_send.at[2 * stage - 1], recv.at[j], peer((p + stage - 1) % 3, 1 + 2 * way),
        )

    def all_here(buffer, recv):
        remote(buffer, buffer, out_send.at[0], recv, sibling).wait_recv()

    def all_gone(buffer, send):
        remote(buffer, buffer, send, last_recv.at[0], sibling).wait_send()

    def send_on(k, digit, columns):
        for p in range(3):
            da, db, dc = digit[p], digit[(p + 1) % 3], digit[(p + 2) % 3]

            if isinstance(da, int):
                da = jnp.int32(da)

            @pl.when(da == 0)
            def _():
                way = jnp.where(dc < 2, 0, 1)
                fwd_copy(1, p, way, k, db * 2 + lax.rem(dc, 2), columns).start()

            @pl.when(((da == 1) & (dc >= 2)) | ((da == 2) & (dc < 2)))
            def _():
                fin_copy(1, p, da - 1, k, db * 4 + dc, columns).start()

    def tiles(half, i, carry):
        columns = pl.ds(128 * half, 128)
        group = group_digits(i)
        at = [y * 16 + x * 4 + z for y, x, z in group]
        for k, digit in zip(at, group):
            acc[k, :, columns] = product(half, *[lax.rem(place[a] + offset(digit[a]), 4) for a in range(3)])
        for k, digit in zip(at, group):
            send_on(k, digit, columns)
        for phase, after in enumerate(TURNS):
            if after // 16 != half:
                continue

            @pl.when(i == after % 16)
            def _():
                d_arrive(phase)
                d_start(phase + 1)

        return carry

    def diagonal_local(b, carry):
        lefts, rights = [], []
        for n in range(2):
            lefts.append(left[2 * b + n])
            high, low = split(strip[2 * b + n])
            rights += [high, low, high, low]
        dfull[...] = dfull[...] + dot(
            jnp.concatenate(lefts, axis=1), jnp.concatenate(rights, axis=0)
        )
        return carry

    py, px, pz = place
    mine = pl.ds(pl.multiple_of(64 * px + 32 * core, 32), 32)

    def d_copies(phase):
        out = []
        if phase in (0, 4):
            for n, (step, flip) in enumerate(around):
                there = 2 * lax.rem(px + step, 4) + (1 - core if flip else core)
                if phase == 0:
                    src, dst = dfull.at[pl.ds(pl.multiple_of(32 * there, 32), 32)], dx.at[n]
                else:
                    src = dst = diagonal_ref.at[mine]
                out.append(remote(src, dst, d_send.at[phase], d_recv.at[phase], plane_peer(step, flip)))
            return out
        for o in (1, 2, 3):
            if phase == 1:
                src, dst, axis = dquarter.at[pl.ds(8 * lax.rem(py + o, 4), 8)], dy.at[o - 1], 0
            elif phase == 2:
                src, dst, axis = dz.at[pz], dz.at[pz], 2
            else:
                part = pl.ds(8 * py, 8)
                src, dst, axis = dquarter2.at[part], dquarter2.at[part], 0
            out.append(remote(src, dst, d_send.at[phase], d_recv.at[phase], peer(axis, o)))
        return out

    def d_bytes(phase):
        return (dx, dy, dz.at[pl.ds(0, 3)], dquarter2.at[pl.ds(0, 24)], diagonal_ref.at[pl.ds(0, 224)])[phase]

    def d_arrive(phase):
        all_here(d_bytes(phase), d_recv.at[phase])
        if phase == 0:
            held = dfull[mine]
            for n in range(len(around)):
                held = held + dx[n]
            dquarter[...] = held
        elif phase == 1:
            dz[pz] = dquarter[pl.ds(8 * py, 8)] + dy[0] + dy[1] + dy[2]
        elif phase == 2:
            dquarter2[pl.ds(8 * py, 8)] = dz[0] + dz[1] + dz[2] + dz[3]
        elif phase == 3:
            diagonal_ref[mine] = dquarter2[...]

    def d_start(phase):
        for copy in d_copies(phase):
            copy.start()

    dfull[...] = jnp.zeros_like(dfull)
    lax.fori_loop(0, blocks // 2, diagonal_local, 0)
    d_start(0)
    across[0].wait_recv()
    across[1].wait_recv()
    weigh(1)
    build(blocks, 1)
    across[2].wait_recv()
    their_table = pltpu.make_async_copy(slots.at[1], table.at[1], load_sem.at[3])
    their_table.start()
    own_table.wait()
    their_table.wait()
    for copy in get_tile:
        copy.wait()
    across[3].wait_recv()
    lax.fori_loop(0, 16, functools.partial(tiles, 0), 0)
    across[4].wait_recv()
    lax.fori_loop(0, 16, functools.partial(tiles, 1), 0)

    def slot(p, da, db, dc):
        digit = [0, 0, 0]
        digit[p], digit[(p + 1) % 3], digit[(p + 2) % 3] = da, db, dc
        return digit[0] * 16 + digit[1] * 4 + digit[2]

    def pass1(j):
        db = j // 2
        all_here(fwd1.at[:, j], fwd1_recv.at[j])
        for p in range(3):
            for way in range(2):
                dc = j % 2 + 2 * way
                k = slot(p, 1 + way, db, dc)
                acc[k, rows_of(p)] = acc[k, rows_of(p)] + fwd1[way, j, rows_of(p)]
                fin_copy(1, p, way, k, db * 4 + dc).start()

    def gather1(f):
        db, dc = f // 4, f % 4
        all_here(fin1.at[:, f], fin1_recv.at[f])
        for p in range(3):
            k = slot(p, 3, db, dc)
            acc[k, rows_of(p)] = acc[k, rows_of(p)] + fin1[0, f, rows_of(p)] + fin1[1, f, rows_of(p)]
            if db == 0:
                fwd_copy(2, p, dc // 2, k, dc % 2).start()
            if db == 1 and dc >= 2:
                fin_copy(2, p, 0, k, dc).start()
            if db == 2 and dc < 2:
                fin_copy(2, p, 1, k, dc).start()

    def pass2(j):
        all_here(fwd2.at[:, j], fwd2_recv.at[j])
        for p in range(3):
            for way in range(2):
                dc = j + 2 * way
                k = slot(p, 3, 1 + way, dc)
                acc[k, rows_of(p)] = acc[k, rows_of(p)] + fwd2[way, j, rows_of(p)]
                fin_copy(2, p, way, k, dc).start()

    def part3(p, way):
        low, size = ROWS[p]
        return (low, CUT) if way == 0 else (low + CUT, size - CUT)

    def fwd3_copy(p, way):
        rows = pl.ds(*part3(p, way))
        return remote(
            acc.at[slot(p, 3, 3, 0), rows], fwd3.at[rows],
            out_send.at[4], last_recv.at[0], peer((p + 2) % 3, 1 + 2 * way),
        )

    def fin3_copy(p, way, half):
        rows = pl.ds(*part3(p, half))
        return remote(
            acc.at[slot(p, 3, 3, 1 + way), rows], fin3.at[way, rows],
            out_send.at[5], last_recv.at[1], peer((p + 2) % 3, 1 + 2 * way),
        )

    def gather2(dc):
        all_here(fin2.at[:, dc], fin2_recv.at[dc])
        for p in range(3):
            k = slot(p, 3, 3, dc)
            acc[k, rows_of(p)] = acc[k, rows_of(p)] + fin2[0, dc, rows_of(p)] + fin2[1, dc, rows_of(p)]
            if dc == 0:
                fwd3_copy(p, 0).start()
                fwd3_copy(p, 1).start()
            if dc == 1:
                fin3_copy(p, 0, 1).start()
            if dc == 2:
                fin3_copy(p, 1, 0).start()

    def pass3():
        all_here(fwd3, last_recv.at[0])
        for p in range(3):
            for way in range(2):
                rows = pl.ds(*part3(p, way))
                k = slot(p, 3, 3, 1 + way)
                acc[k, rows] = acc[k, rows] + fwd3[rows]
                fin3_copy(p, way, way).start()

    def gather3():
        all_here(fin3, last_recv.at[1])
        sum_ref[...] = acc[63] + fin3[0] + fin3[1]

    events = [functools.partial(pass1, j) for j in PASS]
    events += [functools.partial(gather1, f) for f in ORDER[:14]]
    events += [functools.partial(pass2, 0)]
    events += [functools.partial(gather1, f) for f in ORDER[14:]]
    events += [functools.partial(pass2, 1)]
    events += [functools.partial(gather2, dc) for dc in range(4)]
    events += [pass3, gather3]
    for event in events[:EARLY]:
        event()
    d_arrive(4)
    moves = dict(zip(WHEN, events[EARLY:]))
    step = 0
    for _ in factorize(diagonal_ref, factor_ref, inverse_ref):
        step += 1
        if step in moves:
            moves.pop(step)()
    for event in events[EARLY + len(WHEN) - len(moves) :]:
        event()

    for copy in across:
        copy.wait_send()
    for phase in range(5):
        all_gone(d_bytes(phase), d_send.at[phase])
    for n, buffer in enumerate((fwd1, fin1, fwd2, fin2, fwd3, fin3)):
        all_gone(buffer, out_send.at[n])


def finish(factor_ref, inverse_ref, sum_ref, factor_out, update_out):
    factor_out[...] = factor_ref[...]
    update_out[...] = full_dot(inverse_ref[...], sum_ref[...])


def gather_and_sum(weight, count, lists, strip_columns, tiles):
    blocks, width, rows = strip_columns.shape
    items = tiles.shape[0]
    dma = pltpu.SemaphoreType.DMA
    vmem = lambda *shape: pltpu.VMEM(shape, F32)
    any_space = pl.BlockSpec(memory_space=pl.ANY)
    in_vmem = pl.BlockSpec(memory_space=pltpu.VMEM)
    return pl.pallas_call(
        kernel,
        out_shape=[jax.ShapeDtypeStruct((256, 256), F32)] * 3,
        in_specs=[in_vmem, in_vmem, in_vmem, any_space, any_space],
        out_specs=[in_vmem] * 3,
        scratch_shapes=[
            vmem(2 * blocks, width, rows), vmem(2 * blocks, width, rows),
            vmem(2 * items, width, 128), vmem(2 * items, width, 128),
            pltpu.VMEM((2 * blocks + 2, rows, 4 * width), jnp.bfloat16),
            vmem(2, width, 128), pltpu.VMEM((2, 2, 128), jnp.int32), pltpu.SMEM((2, 2, 128), jnp.int32),
            vmem(64, 256, 256),
            vmem(2, 8, 256, 256), vmem(2, 16, 256, 256), vmem(2, 2, 256, 256), vmem(2, 4, 256, 256),
            vmem(256, 256), vmem(2, 256, 256),
            vmem(256, 256),
            vmem(256, 256), vmem(7, 32, 256), vmem(32, 256),
            vmem(3, 8, 256), vmem(4, 8, 256), vmem(32, 256),
            dma((5,)), dma((5,)), dma((5,)),
            dma((8,)), dma((16,)), dma((2,)), dma((4,)), dma((6,)), dma((2,)),
            dma((5,)), dma((5,)),
        ],
        compiler_params=pltpu.CompilerParams(
            collective_id=0, has_side_effects=True, vmem_limit_bytes=60 << 20
        ),
    )(weight, count, lists, strip_columns, tiles)


def per_device(strip_columns, tile_columns, barrier_weights, column_counts, tile_lists):
    blocks, touched, width, own_width = tile_columns.shape
    in_vmem = pl.BlockSpec(memory_space=pltpu.VMEM)
    parts = gather_and_sum(
        barrier_weights,
        column_counts.reshape(1, blocks),
        tile_lists.T,
        strip_columns,
        tile_columns.reshape(blocks * touched, width, own_width),
    )
    return pl.pallas_call(
        finish,
        out_shape=[jax.ShapeDtypeStruct((256, 256), F32)] * 2,
        in_specs=[in_vmem] * 3,
        out_specs=[in_vmem] * 2,
    )(*parts)


def solution(mesh):
    return jax.shard_map(
        per_device,
        mesh=mesh,
        in_specs=(
            P(AXES, None, None),
            P(AXES, None, None, None),
            P(AXES, None),
            P(AXES),
            P(AXES, None),
        ),
        out_specs=(P(), P(None, AXES)),
        check_vma=False,
    )
```
